128 devices in a mesh: cluster: 4 (over y), sub: 32 (over x, z, core).
Axes of the slice: x: 4, y: 4, z: 4, core: 2. Of those that a mesh axis runs over, the one named last changes fastest.
Arguments:
- factor_tiles: float32 [128, 300, 128, 128], P(('cluster', 'sub')), may hold values from -1 to 2, as said below
- rigid_modes: float32 [128, 6, 3072], P(('cluster', 'sub')), may hold values from -6 to 6
- load_cases: float32 [128, 32, 3072], P(('cluster', 'sub')), may hold values from -6 to 6
- coarse_load: float32 [24, 32], replicated, may hold values from -20480 to 20480
- peer_slots: int32 [128, 128, 96], P(('cluster', 'sub')), may hold values from 0 to 640, as said below
- slot_unknown: int32 [128, 640], P(('cluster', 'sub')), may hold values from 0 to 3072, as said below
Outputs:
- multipliers: float32 [128, 640, 32], P(('cluster', 'sub'))
- projected: float32 [128, 640, 32], P(('cluster', 'sub'))
The draws below stay inside these ranges and needn't reach their ends.
Inputs may be any that keep to these rules, and one draw needn't show every extreme that they name: For k below the number of multipliers shared by subdomains a and b, peer_slots[a, b, k] is the slot of a holding the k-th of them, in the same order as peer_slots[b, a, k]; other places hold 640; each slot is listed at most once in peer_slots[a]; a shares multipliers only with the subdomain of the same index within the next or previous cluster (at most 96) and with subdomains of its own cluster whose grid positions differ from its own by at most one in each coordinate, where index w within a cluster stands at z = w // (32 / 2), x = (w % (32 / 2)) // 4, y = w % 4; such a pair shares at most 96 multipliers if the positions differ in one coordinate, at most 12 if in two, at most 3 if in three; some pair shares exactly 96, some pair differing in two coordinates exactly 12. `slot_unknown`: distinct over the listed slots of one subdomain; exactly 3072 on the slots that peer_slots[s] does not list, and every subdomain has such slots. `factor_tiles`: tiles with I = J are lower triangular with diagonal entries from 1 to 2.
All inputs are finite; a program needn't handle non-finite values.
Results may differ from the reference program's by a relative error of at most 0.0003.
Values sent between devices are 32-bit elements; how exact they have to be, the bound alone decides.
No kernel may reach another device: no remote copies, remote signals or barrier semaphores. Data moves between devices by JAX's collectives and lax.ppermute only.
A program may use at most 320 MiB of HBM per device.

```python
import math
import jax
import jax.numpy as jnp
import numpy as np
from jax import lax

UNKNOWNS = 3072
SLOTS = 640
TILE = 128
MODES = 6
PAIR_MOST = 96
LOADS = 32
ITERS = 2
TILE_ROWS = 24
TILES = 300
SUBS = 128
COARSE = 24
N_CLUSTER = 4
N_SUB = 32


def cluster_geometry():
    breadth_y = 2 + 2 * min(1, N_SUB // 32)
    half_count = N_SUB // 2
    device_ids = np.arange(SUBS)
    cluster_of = device_ids // N_SUB
    within = device_ids % N_SUB
    breadth_x = half_count // breadth_y
    coord_z = within // half_count
    coord_y = within % breadth_y
    coord_x = within % half_count // breadth_y
    delta_x = np.abs(coord_x[:, None] - coord_x[None, :])
    delta_y = np.abs(coord_y[:, None] - coord_y[None, :])
    delta_z = np.abs(coord_z[:, None] - coord_z[None, :])
    same = cluster_of[:, None] == cluster_of[None, :]
    nearby = same & (delta_x <= 1) & (delta_y <= 1) & (delta_z <= 1)
    kinds = np.where(nearby, delta_x + delta_y + delta_z, 0)
    boundary = np.where(cluster_of % 2 == 0, breadth_x - 1, 0)
    crossing = (cluster_of[None, :] == cluster_of[:, None] + 1) & (within[:, None] == within[None, :]) & (coord_x[:, None] == boundary[:, None])
    crossing = crossing | crossing.T
    return np.where(crossing, 1, kinds).astype(np.int32)


def node_pick(subkey):
    return jax.random.permutation(subkey, UNKNOWNS)[:SLOTS]


def draw_topology(key):
    kinds = jnp.asarray(cluster_geometry())
    breadth_y = 2 + 2 * min(1, N_SUB // 32)
    edge_most = 3 * max(2, PAIR_MOST // 24)
    face_key, edge_key, node_key = jax.random.split(jax.random.fold_in(key, 7), 3)
    upper = jnp.asarray(np.triu(np.ones((SUBS, SUBS), bool), 1))
    face = 3 * jax.random.randint(face_key, (SUBS, SUBS), PAIR_MOST // 6, PAIR_MOST // 3 + 1)
    face = jnp.where(upper, face, face.T)
    edge = 3 * jax.random.randint(edge_key, (SUBS, SUBS), 1, max(2, PAIR_MOST // 24) + 1)
    edge = jnp.where(upper, edge, edge.T)
    counts = jnp.where(kinds == 1, face, jnp.where(kinds == 2, edge, jnp.where(kinds == 3, 3, 0)))
    counts = counts.at[0, 1].set(PAIR_MOST).at[1, 0].set(PAIR_MOST)
    counts = counts.at[0, breadth_y + 1].set(edge_most).at[breadth_y + 1, 0].set(edge_most)
    offsets = jnp.cumsum(counts, axis=1) - counts
    places = jnp.arange(PAIR_MOST, dtype=jnp.int32)
    table = jnp.where(places[None, None, :] < counts[:, :, None], offsets[:, :, None] + places[None, None, :], SLOTS)
    totals = jnp.sum(counts, axis=1)
    picks = jax.vmap(node_pick)(jax.random.split(node_key, SUBS))
    nodes = jnp.where(jnp.arange(SLOTS)[None, :] < totals[:, None], picks, UNKNOWNS)
    return (table.astype(jnp.int32), nodes.astype(jnp.int32))


def draw_peer_slots(key, part):
    return draw_topology(key)[0]


def draw_slot_unknown(key, part):
    return draw_topology(key)[1]


def draw_factor_tiles(key, part):
    diagonal_flags = np.zeros(TILES, bool)
    for tile_row in range(TILE_ROWS):
        diagonal_flags[tile_row * (tile_row + 1) // 2 + tile_row] = True
    noise_key, scale_key = jax.random.split(key)
    shape = (SUBS, TILES, TILE, TILE)
    noise = jax.random.normal(noise_key, shape, jnp.float32)
    noise = noise * (0.3 / math.sqrt(UNKNOWNS))
    diagonal = jnp.exp(jax.random.uniform(scale_key, (SUBS, TILES, TILE), jnp.float32, 0.0, math.log(2.0)))
    lower = jnp.asarray(np.tril(np.ones((TILE, TILE), np.float32), -1))
    identity = jnp.asarray(np.eye(TILE, dtype=np.float32))
    diagonal_tiles = noise * lower + identity * diagonal[:, :, None, :]
    return jnp.where(jnp.asarray(diagonal_flags)[None, :, None, None], diagonal_tiles, noise)


def block_levels(own_key, shape, shards, least, high):
    level = 1.0
    for position, blocks in shards:
        draws = jax.random.uniform(jax.random.fold_in(jax.random.fold_in(own_key, 6), position), (blocks,), jnp.float32, least / len(shards), high / len(shards))
        level = level * jnp.repeat(jnp.exp(draws), shape[position] // blocks).reshape((-1,) + (1,) * (len(shape) - 1 - position))
    return level


def bell_draw(rng, extent, scale, bound, cuts=(), held_as=jnp.bfloat16):
    loudness = block_levels(rng, extent, cuts, -0.22, 0.18) if cuts else 1.0
    drawn = jax.random.normal(rng, extent, jnp.float32) * scale * loudness
    return jnp.minimum(jnp.maximum(drawn, -bound), bound).astype(held_as)


def setup_inputs(seed: int = 0) -> dict:
    key_of = jax.random.split(jax.random.key(seed), 7)
    return {
        "factor_tiles": draw_factor_tiles(jax.random.fold_in(key_of[6], 71), 0),
        "rigid_modes": bell_draw(key_of[1], (SUBS, MODES, UNKNOWNS), 1.0, 6.0, ((0, 128),), jnp.float32),
        "load_cases": bell_draw(key_of[2], (SUBS, LOADS, UNKNOWNS), 1.0, 6.0, ((0, 128),), jnp.float32),
        "coarse_load": bell_draw(key_of[3], (COARSE, LOADS), (100 * N_SUB), 20480.0, (), jnp.float32),
        "peer_slots": draw_peer_slots(jax.random.fold_in(key_of[6], 71), 0),
        "slot_unknown": draw_slot_unknown(jax.random.fold_in(key_of[6], 71), 0),
    }


HIGH = lax.Precision.HIGHEST

def unpack(tiles):
    count = tiles.shape[0]
    tile_edge = tiles.shape[1]
    blocks = (math.isqrt(8 * count + 1) - 1) // 2
    stacked = []
    for tile_row in range(blocks):
        pieces = [tiles[tile_row * (tile_row + 1) // 2 + tile_col] for tile_col in range(tile_row + 1)]
        if tile_row + 1 < blocks:
            pieces.append(jnp.zeros((tile_edge, tile_edge * (blocks - tile_row - 1)), tiles.dtype))
        stacked.append(jnp.concatenate(pieces, axis=1))
    return jnp.concatenate(stacked, axis=0)

def local_setup(tiles, rigid_rows, forces, slot_nodes, slot_signs, membership):
    factor = unpack(tiles)
    unknowns = factor.shape[0]
    slot_count = slot_nodes.shape[0]
    gluing = (jnp.arange(unknowns, dtype=jnp.int32)[:, None] == slot_nodes[None, :]).astype(jnp.float32) * slot_signs[None, :]
    solved = jax.scipy.linalg.solve_triangular(factor, jnp.concatenate([gluing, forces.T], axis=1), lower=True)
    spread = solved[:, :slot_count]
    settled = solved[:, slot_count:]
    dual_matrix = jnp.dot(spread.T.astype(jnp.float32), spread.astype(jnp.float32), precision=HIGH, preferred_element_type=jnp.float32)
    dual_load = jnp.dot(spread.T.astype(jnp.float32), settled.astype(jnp.float32), precision=HIGH, preferred_element_type=jnp.float32)
    local_modes = jnp.dot(gluing.T.astype(jnp.float32), rigid_rows.T.astype(jnp.float32), precision=HIGH, preferred_element_type=jnp.float32)
    half_modes = (local_modes[:, None, :] * membership[None, :, None]).reshape(slot_count, -1)
    return (dual_matrix, dual_load, half_modes)

def reference(factor_tiles, rigid_modes, load_cases, coarse_load, peer_slots, slot_unknown):
    subdomains = peer_slots.shape[0]
    peer_order = jnp.arange(subdomains, dtype=jnp.int32)
    upward = jnp.where(peer_order[None, :] > peer_order[:, None], 1.0, -1.0).astype(jnp.float32)
    slot_signs = jnp.zeros((subdomains, SLOTS + 1), jnp.float32).at[peer_order[:, None, None], peer_slots].add(jnp.broadcast_to(upward[:, :, None], peer_slots.shape))[:, :SLOTS]
    membership = (peer_order[:, None] // N_SUB == jnp.arange(N_CLUSTER, dtype=jnp.int32)[None, :]).astype(jnp.float32)

    def setup_one(arrays):
        return local_setup(*arrays)
    dual_matrix, dual_load, half_modes = lax.map(setup_one, (factor_tiles, rigid_modes, load_cases, slot_unknown, slot_signs, membership))

    def pair(values):
        breadth = values.shape[2]
        extended = jnp.concatenate([values, jnp.zeros((subdomains, 1, breadth), values.dtype)], axis=1)

        def incoming(target):
            sources = lax.dynamic_index_in_dim(peer_slots, target, 1, keepdims=False)
            received = extended[peer_order[:, None], sources]
            own_slots = lax.dynamic_index_in_dim(peer_slots, target, 0, keepdims=False)
            summed = jnp.zeros((SLOTS + 1, breadth), values.dtype).at[own_slots.reshape(-1)].add(received.reshape(-1, breadth))
            return summed[:SLOTS]
        return values + lax.map(incoming, peer_order)
    modes = pair(half_modes)
    coarse_gram = 0.5 * jnp.einsum('sjc,sjd->cd', modes, modes, precision=HIGH)
    coarse_factor = jnp.linalg.cholesky(coarse_gram)

    def project(values):
        coarse = 0.5 * jnp.einsum('sjc,sjl->cl', modes, values, precision=HIGH)
        weights = jax.scipy.linalg.cho_solve((coarse_factor, True), coarse)
        return values - jnp.einsum('sjc,cl->sjl', modes, weights, precision=HIGH)

    def apply_dual(values):
        return jnp.einsum('sij,sjl->sil', dual_matrix, values, precision=HIGH)
    start_weights = jax.scipy.linalg.cho_solve((coarse_factor, True), coarse_load)
    multipliers = jnp.einsum('sjc,cl->sjl', modes, start_weights, precision=HIGH)
    residual = pair(dual_load - apply_dual(multipliers))
    projected = project(residual)
    current = 0.5 * lax.optimization_barrier(jnp.sum(projected * projected, axis=(0, 1)))
    direction = projected
    for iteration in range(ITERS):
        image = pair(apply_dual(direction))
        alpha = current / (0.5 * lax.optimization_barrier(jnp.sum(direction * image, axis=(0, 1))))
        multipliers = multipliers + alpha * direction
        residual = residual - alpha * image
        projected = project(residual)
        following = 0.5 * lax.optimization_barrier(jnp.sum(projected * projected, axis=(0, 1)))
        direction = projected + following / current * direction
        current = following
    return (multipliers, projected)
```

```python
import functools

import jax
import jax.numpy as jnp
from jax import lax
from jax.experimental import pallas as pl
from jax.experimental.pallas import tpu as pltpu
from jax.sharding import PartitionSpec as P

F32 = jnp.float32
BF16 = jnp.bfloat16
HIGH = lax.Precision.HIGHEST

UNKNOWNS = 3072
SLOTS = 640
LOADS = 32
RHS = SLOTS + LOADS
TILE = 128
TILE_ROWS = 24
BLOCK = 256
BLOCKS = UNKNOWNS // BLOCK
SUBS = 32
CLUSTERS = 4
MODES = 6
LANES = 128
COARSE_AT = 96
OFFSETS = [
    (dz, dx, dy)
    for dz in (0, 1)
    for dx in (-1, 0, 1)
    for dy in (-1, 0, 1)
    if (dz, dx, dy) != (0, 0, 0)
]
PEERS = len(OFFSETS) + 2
LOWER, UPPER, NOBODY = SUBS, SUBS + 1, SUBS + 2
TABLE_ROWS = 40
VMEM = pl.BlockSpec(memory_space=pltpu.VMEM)
SMEM = pl.BlockSpec(memory_space=pltpu.SMEM)
ANY = pl.BlockSpec(memory_space=pl.ANY)


def nt(a, b, precision=None):
    return lax.dot_general(
        a, b, (((1,), (1,)), ((), ())), precision=precision, preferred_element_type=F32
    )


def nn(a, b, precision=None):
    return lax.dot_general(
        a, b, (((1,), (0,)), ((), ())), precision=precision, preferred_element_type=F32
    )


def halves(a):
    high = a.astype(BF16)
    return high, (a - high.astype(F32)).astype(BF16)


def thirds(a):
    high = a.astype(BF16)
    rest = a - high.astype(F32)
    middle = rest.astype(BF16)
    return jnp.concatenate([high, middle, (rest - middle.astype(F32)).astype(BF16)], axis=0)


def fold(a, rows):
    return a[:rows] + a[rows : 2 * rows] + a[2 * rows :]


def mm3(a, b):
    ah, al = halves(a)
    bh, bl = halves(b)
    return nn(jnp.concatenate([ah, al, ah], axis=1), jnp.concatenate([bh, bh, bl], axis=0))


def peers_of(me):
    z, x, y = me // 16, (me // 4) % 4, me % 4
    found = []
    for dz, dx, dy in OFFSETS:
        to_z = 1 - z if dz else z
        to_x, to_y = x + dx, y + dy
        valid = (to_x >= 0) & (to_x < 4) & (to_y >= 0) & (to_y < 4)
        found.append((valid, jnp.where(valid, to_z * 16 + to_x * 4 + to_y, me)))
    return found


def select_slots(table, me, picks):
    slot = lax.broadcasted_iota(jnp.int32, (SLOTS, LANES), 0)
    rows = [jnp.where(valid, peer, NOBODY) for valid, peer in peers_of(me)] + [LOWER, UPPER]
    for place, row in enumerate(rows):
        wanted = table[pl.ds(row, 1), :]
        picks[:, place * LANES : (place + 1) * LANES] = jnp.where(slot == wanted, 1.0, 0.0).astype(
            BF16
        )


def send_values(values, extra, me, picks, to_sub, to_lower, to_upper):
    for peer in range(SUBS):
        to_sub[peer] = extra
    picked = fold(nn(thirds(values), picks[...]), LOADS)
    for place, (valid, peer) in enumerate(peers_of(me)):

        @pl.when(valid)
        def _():
            to_sub[peer] = picked[:, place * LANES : (place + 1) * LANES] + extra

    to_lower[...] = picked[:, (PEERS - 2) * LANES : (PEERS - 1) * LANES]
    to_upper[...] = picked[:, (PEERS - 1) * LANES :]


def received_sum(me, picks, sub, lower, upper):
    pieces = [sub[peer] for _, peer in peers_of(me)] + [lower[...], upper[...]]
    return fold(nt(thirds(jnp.concatenate(pieces, axis=1)), picks[...]), LOADS)


def prepare_kernel(
    where, table, unknown, rigid, signs, half, to_sub, to_lower, to_upper, picks
):
    me, cluster = where[0], where[1]
    select_slots(table, me, picks)
    sign = jnp.zeros((SLOTS, LANES), F32)
    ups = [jnp.where(peer > me, 1.0, -1.0) for _, peer in peers_of(me)] + [-1.0, 1.0]
    for place, up in enumerate(ups):
        sign = sign + picks[:, place * LANES : (place + 1) * LANES].astype(F32) * up
    sign = jnp.sum(sign, axis=1, keepdims=True)
    signs[...] = sign
    own = jnp.zeros((3 * MODES + 6, SLOTS), F32)
    lane = lax.broadcasted_iota(jnp.int32, (SLOTS, BLOCK), 1)
    for block in range(BLOCKS):
        rows = rigid[:, block * BLOCK : (block + 1) * BLOCK]
        rows = jnp.concatenate([rows, jnp.zeros((2, BLOCK), F32)], axis=0)
        glue = jnp.where(unknown[...] - block * BLOCK == lane, sign, 0.0).astype(BF16)
        own = own + nt(thirds(rows), glue)
    own = fold(own, 8)
    row = lax.broadcasted_iota(jnp.int32, (LOADS, SLOTS), 0)
    placed = jnp.zeros((LOADS, SLOTS), F32)
    for mode in range(MODES):
        placed = jnp.where(row == cluster * MODES + mode, own[mode : mode + 1, :], placed)
    half[...] = placed
    send_values(placed, jnp.zeros((LOADS, LANES), F32), me, picks, to_sub, to_lower, to_upper)


def modes_kernel(where, table, half, sub, lower, upper, modes, gram, picks):
    select_slots(table, where[0], picks)
    total = half[...] + received_sum(where[0], picks, sub, lower, upper)
    modes[...] = jnp.concatenate([jnp.zeros((COARSE_AT, SLOTS), F32), total], axis=0)
    gram[...] = 0.5 * nt(total, total, HIGH)


def invert_kernel(tiles, high, low, diag, beside, inverse, sems):
    copies = []
    for t in range(TILE_ROWS):
        copies.append(
            pltpu.make_async_copy(tiles.at[t * (t + 1) // 2 + t], diag.at[t], sems.at[t])
        )
    for j in range(BLOCKS):
        t = 2 * j + 1
        copies.append(
            pltpu.make_async_copy(
                tiles.at[t * (t + 1) // 2 + t - 1], beside.at[j], sems.at[TILE_ROWS + j]
            )
        )
    for copy in copies:
        copy.start()
    for copy in copies:
        copy.wait()
    base = 16
    count = TILE // base
    lane3 = lax.broadcasted_iota(jnp.int32, (TILE_ROWS, base, TILE), 2)
    row3 = lax.broadcasted_iota(jnp.int32, (TILE_ROWS, base, TILE), 1)
    compact = jnp.zeros((TILE_ROWS, base, TILE), F32)
    for b in range(count):
        compact = jnp.where(lane3 // base == b, diag[:, b * base : (b + 1) * base, :], compact)
    parts = thirds(compact.reshape(TILE_ROWS * base, TILE))
    lane = lax.broadcasted_iota(jnp.int32, (TILE, TILE), 1)
    row = lax.broadcasted_iota(jnp.int32, (TILE, TILE), 0)
    solved = jnp.where(row3 == lane3 % base, 1.0, 0.0)
    for k in range(base):
        spread = jnp.where(row == (lane // base) * base + k, 1.0, 0.0).astype(BF16)
        column = fold(nn(parts, spread), TILE_ROWS * base).reshape(TILE_ROWS, base, TILE)
        pivot = solved[:, k : k + 1, :] / column[:, k : k + 1, :]
        solved = jnp.where(
            row3 == k, pivot, jnp.where(row3 > k, solved - column * pivot, solved)
        )
    for b in range(count):
        inverse[:, b * base : (b + 1) * base, :] = jnp.where(lane3 // base == b, solved, 0.0)
    size = base
    while size < TILE:
        below = ((row // size) % 2 == 1) & (lane // size == row // size - 1)
        for t in range(TILE_ROWS):
            now = inverse[t]
            inverse[t] = now - mm3(now, mm3(jnp.where(below, diag[t], 0.0), now))
        size *= 2
    for j in range(BLOCKS):
        first, second = inverse[2 * j], inverse[2 * j + 1]
        off = -mm3(second, mm3(beside[j], first))
        whole = jnp.concatenate(
            [
                jnp.concatenate([first, jnp.zeros((TILE, TILE), F32)], axis=1),
                jnp.concatenate([off, second], axis=1),
            ],
            axis=0,
        )
        high[j], low[j] = halves(whole)


def solve_kernel(
    tiles, high, low, unknown, signs, loads, dual, load, held, xh, xl, total, sems
):
    copies = []
    for i in range(BLOCKS):
        first, count = i * (2 * i + 1), 4 * i + 3
        copies.append(
            pltpu.make_async_copy(
                tiles.at[pl.ds(first, count)], held.at[pl.ds(first, count)], sems.at[i]
            )
        )
    for copy in copies:
        copy.start()
    lane = lax.broadcasted_iota(jnp.int32, (SLOTS, BLOCK), 1)
    for i in range(BLOCKS):
        copies[i].wait()
        first = i * (2 * i + 1)
        total[:SLOTS, :] = jnp.where(unknown[...] - i * BLOCK == lane, signs[...], 0.0)
        total[SLOTS:, :] = loads[:, i * BLOCK : (i + 1) * BLOCK]

        def step(k, carry):
            upper, under = first + 2 * k, first + 2 * i + 1 + 2 * k
            tile = jnp.concatenate(
                [
                    jnp.concatenate([held[upper], held[upper + 1]], axis=1),
                    jnp.concatenate([held[under], held[under + 1]], axis=1),
                ],
                axis=0,
            )
            th, tl = halves(tile)
            at = pl.ds(pl.multiple_of(k * BLOCK, BLOCK), BLOCK)
            ah, al = xh[:, at], xl[:, at]
            total[...] -= nt(
                jnp.concatenate([ah, al, ah], axis=1), jnp.concatenate([th, th, tl], axis=1)
            )
            return carry

        if i:
            lax.fori_loop(0, i, step, 0)
        ah, al = halves(total[...])
        solved = nt(
            jnp.concatenate([ah, al, ah], axis=1),
            jnp.concatenate([high[i], high[i], low[i]], axis=1),
        )
        at = slice(i * BLOCK, (i + 1) * BLOCK)
        xh[:, at], xl[:, at] = halves(solved)

    dual[...] = jnp.zeros_like(dual)
    load[...] = jnp.zeros_like(load)

    def gather(k, carry):
        at = pl.ds(pl.multiple_of(k * BLOCK, BLOCK), BLOCK)
        ah, al = xh[:, at], xl[:, at]
        product = nt(
            jnp.concatenate([ah, al, ah], axis=1),
            jnp.concatenate([ah[:SLOTS], ah[:SLOTS], al[:SLOTS]], axis=1),
        )
        dual[...] += product[:SLOTS]
        load[...] += product[SLOTS:]
        return carry

    lax.fori_loop(0, BLOCKS, gather, 0)


def gram_inverse(gram):
    row = lax.broadcasted_iota(jnp.int32, (LOADS, LANES), 0)
    lane = lax.broadcasted_iota(jnp.int32, (LOADS, LANES), 1)
    filled = jnp.concatenate([gram, jnp.zeros((LOADS, LANES - LOADS), F32)], axis=1)
    filled = jnp.where((row >= CLUSTERS * MODES) & (row == lane), 1.0, filled)
    filled = jnp.where(lane == row + LOADS, 1.0, filled)
    for k in range(CLUSTERS * MODES):
        pivot = filled[k : k + 1, :] / filled[k : k + 1, k : k + 1]
        factor = jnp.where(row[:, :1] > k, filled[:, k : k + 1], 0.0)
        filled = filled - factor * pivot
    scale = jnp.sum(jnp.where(row == lane, filled, 0.0), axis=1, keepdims=True)
    lower = jnp.where((lane >= LOADS) & (lane < 2 * LOADS) & (row < CLUSTERS * MODES), filled, 0.0)
    lower = lower * lax.rsqrt(scale)
    lower = pltpu.roll(lower, COARSE_AT - LOADS, 1)
    return lax.dot_general(
        lower, lower, (((0,), (0,)), ((), ())), precision=HIGH, preferred_element_type=F32
    )


def coarse_lanes(values):
    lane = lax.broadcasted_iota(jnp.int32, values.shape, 1)
    return jnp.where((lane >= COARSE_AT) & (lane < COARSE_AT + CLUSTERS * MODES), values, 0.0)


def with_scalars(values, *scalars):
    lane = lax.broadcasted_iota(jnp.int32, values.shape, 1)
    values = coarse_lanes(values)
    for place, scalar in enumerate(scalars):
        values = jnp.where(lane == COARSE_AT + CLUSTERS * MODES + place, scalar, values)
    return values


def scalar(values, place):
    at = COARSE_AT + CLUSTERS * MODES + place
    return values[:, at : at + 1]


def rows_sum(a, b):
    return jnp.sum(a * b, axis=1, keepdims=True)


def start_kernel(
    where, table, gram, coarse_load, modes, dual, load,
    inverse, multipliers, values, to_sub, to_lower, to_upper, picks,
):
    select_slots(table, where[0], picks)
    inverse[...] = gram_inverse(gram[...])
    weights = nn(coarse_load[...], inverse[...], HIGH)
    multipliers[...] = nn(weights, modes[...], HIGH)
    values[...] = load[...] - nn(multipliers[...], dual[...], HIGH)
    extra = with_scalars(nt(values[...], modes[...], HIGH))
    send_values(values[...], extra, where[0], picks, to_sub, to_lower, to_upper)


def pair_kernel(where, table, values, sub, lower, upper, paired, picks):
    select_slots(table, where[0], picks)
    paired[...] = values[...] + received_sum(where[0], picks, sub, lower, upper)


def first_kernel(
    where, table, s0, s1, s2, s3, inverse, modes, dual, residual,
    projected, values, to_sub, to_lower, to_upper, picks,
):
    select_slots(table, where[0], picks)
    sums = (s0[...] + s1[...]) + (s2[...] + s3[...])
    weights = nn(coarse_lanes(sums), inverse[...], HIGH)
    projected[...] = residual[...] - nn(weights, modes[...], HIGH)
    values[...] = nn(projected[...], dual[...], HIGH)
    extra = with_scalars(
        nt(values[...], modes[...], HIGH),
        0.5 * rows_sum(projected[...], projected[...]),
        rows_sum(projected[...], values[...]),
    )
    send_values(values[...], extra, where[0], picks, to_sub, to_lower, to_upper)


def second_kernel(
    where, table, s0, s1, s2, s3, inverse, modes, dual, image, multipliers, projected,
    sums, moved, newer, values, to_sub, to_lower, to_upper, picks,
):
    select_slots(table, where[0], picks)
    sums[...] = (s0[...] + s1[...]) + (s2[...] + s3[...])
    alpha = scalar(sums, 0) / scalar(sums, 1)
    weights = nn(coarse_lanes(sums[...]), inverse[...], HIGH)
    moved[...] = multipliers[...] + alpha * projected[...]
    newer[...] = projected[...] - alpha * (image[...] - nn(weights, modes[...], HIGH))
    values[...] = nn(newer[...], dual[...], HIGH)
    extra = with_scalars(
        nt(values[...], modes[...], HIGH),
        0.5 * rows_sum(newer[...], newer[...]),
        rows_sum(newer[...], values[...]),
        0.5 * rows_sum(newer[...], image[...]),
    )
    send_values(values[...], extra, where[0], picks, to_sub, to_lower, to_upper)


def last_kernel(
    s0, s1, s2, s3, before, inverse, modes, paired, image, moved, projected, newer,
    multipliers_out, projected_out,
):
    sums = (s0[...] + s1[...]) + (s2[...] + s3[...])
    following = scalar(sums, 0)
    beta = following / scalar(before, 0)
    curvature = scalar(sums, 1) + beta * (2.0 * scalar(sums, 2) + beta * scalar(before, 1))
    alpha = following / curvature
    direction = newer[...] + beta * projected[...]
    image_now = paired[...] + beta * image[...]
    coarse = coarse_lanes(sums + beta * before[...])
    weights = nn(coarse, inverse[...], HIGH)
    multipliers_out[...] = jnp.transpose(moved[...] + alpha * direction)
    projected_out[...] = jnp.transpose(
        newer[...] - alpha * (image_now - nn(weights, modes[...], HIGH))
    )


def shape(*dims, dtype=F32):
    return jax.ShapeDtypeStruct(dims, dtype)


SENT = (shape(SUBS, LOADS, LANES), shape(LOADS, LANES), shape(LOADS, LANES))
VECTOR = shape(LOADS, SLOTS)
PICKS = pltpu.VMEM((SLOTS, PEERS * LANES), BF16)


def call(kernel, out_shape, in_specs, scratch, flops, moved, name, limit=24):
    return pl.pallas_call(
        kernel,
        out_shape=out_shape,
        in_specs=in_specs,
        out_specs=jax.tree.map(lambda _: VMEM, out_shape),
        scratch_shapes=scratch,
        cost_estimate=pl.CostEstimate(flops=flops, bytes_accessed=moved, transcendentals=0),
        compiler_params=pltpu.CompilerParams(vmem_limit_bytes=limit << 20),
        name=name,
    )


def exchange(sent):
    to_sub, to_lower, to_upper = sent
    up = [(c, c + 1) for c in range(CLUSTERS - 1)]
    down = [(c + 1, c) for c in range(CLUSTERS - 1)]
    from_lower = lax.ppermute(to_upper, "cluster", up)
    from_upper = lax.ppermute(to_lower, "cluster", down)
    received = lax.all_to_all(to_sub, "sub", split_axis=0, concat_axis=0, tiled=True)
    return received, from_lower, from_upper


def cluster_sums(received):
    own = jnp.sum(received, axis=0)
    others = [
        lax.ppermute(own, "cluster", [(c, (c + by) % CLUSTERS) for c in range(CLUSTERS)])
        for by in (1, 2, 3)
    ]
    return (own, *others)


def local(factor_tiles, rigid_modes, load_cases, coarse_load, peer_slots, slot_unknown):
    cluster = lax.axis_index("cluster")
    me = lax.axis_index("sub")
    own = cluster * SUBS + me
    devices = CLUSTERS * SUBS
    places = peer_slots[0]
    inner = lax.dynamic_slice_in_dim(places, cluster * SUBS, SUBS, 0)
    lower, upper = own - SUBS, own + SUBS
    low_row = jnp.where(lower >= 0, places[jnp.maximum(lower, 0)], SLOTS)
    up_row = jnp.where(upper < devices, places[jnp.minimum(upper, devices - 1)], SLOTS)
    table = jnp.concatenate([inner, low_row[None], up_row[None]], axis=0)
    table = jnp.pad(
        table,
        ((0, TABLE_ROWS - SUBS - 2), (0, LANES - table.shape[1])),
        constant_values=SLOTS,
    )
    where = jnp.stack([me, cluster]).astype(jnp.int32)
    unknown = slot_unknown[0][:, None]
    tiles = factor_tiles[0]
    small = 1 << 22

    signs, half, *sent = call(
        prepare_kernel,
        (shape(SLOTS, 1), VECTOR, *SENT),
        [SMEM, VMEM, VMEM, VMEM],
        [PICKS], 1 << 30, small, "prepare",
    )(where, table, unknown, rigid_modes[0])
    received = exchange(sent)

    high, low = call(
        invert_kernel,
        (shape(BLOCKS, BLOCK, BLOCK, dtype=BF16),) * 2,
        [ANY],
        [
            pltpu.VMEM((TILE_ROWS, TILE, TILE), F32),
            pltpu.VMEM((BLOCKS, TILE, TILE), F32),
            pltpu.VMEM((TILE_ROWS, TILE, TILE), F32),
            pltpu.SemaphoreType.DMA((TILE_ROWS + BLOCKS,)),
        ],
        10 << 30, small, "invert", 40,
    )(tiles)

    modes, gram = call(
        modes_kernel,
        (shape(LANES, SLOTS), shape(LOADS, LOADS)),
        [SMEM] + [VMEM] * 5,
        [PICKS], 1 << 30, small, "modes",
    )(where, table, half, *received)
    gram = jnp.broadcast_to(gram.reshape(1, 8, LANES), (devices, 8, LANES))
    gram = lax.all_to_all(gram, ("cluster", "sub"), split_axis=0, concat_axis=0, tiled=True)

    dual, load = call(
        solve_kernel,
        (shape(SLOTS, SLOTS), VECTOR),
        [ANY] + [VMEM] * 5,
        [
            pltpu.VMEM(tiles.shape, F32),
            pltpu.VMEM((RHS, UNKNOWNS), BF16),
            pltpu.VMEM((RHS, UNKNOWNS), BF16),
            pltpu.VMEM((RHS, BLOCK), F32),
            pltpu.SemaphoreType.DMA((BLOCKS,)),
        ],
        60 << 30, 5 * small, "solve", 56,
    )(tiles, high, low, unknown, signs, load_cases[0])
    gram = jnp.sum(gram, axis=0).reshape(LOADS, LOADS)

    spread_load = jnp.pad(
        coarse_load.T, ((0, 0), (COARSE_AT, LANES - COARSE_AT - CLUSTERS * MODES))
    )
    inverse, multipliers, values, *sent = call(
        start_kernel,
        (shape(LANES, LANES), VECTOR, VECTOR, *SENT),
        [SMEM] + [VMEM] * 6,
        [PICKS], 1 << 30, small, "start",
    )(where, table, gram, spread_load, modes, dual, load)

    def meet(values, sent):
        received = exchange(sent)
        sums = cluster_sums(received[0])
        paired = call(
            pair_kernel, VECTOR, [SMEM] + [VMEM] * 5, [PICKS], 1 << 30, small, "pair"
        )(where, table, values, *received)
        return sums, paired

    sums, residual = meet(values, sent)
    projected, values, *sent = call(
        first_kernel,
        (VECTOR, VECTOR, *SENT),
        [SMEM] + [VMEM] * 9,
        [PICKS], 1 << 30, small, "first",
    )(where, table, *sums, inverse, modes, dual, residual)
    sums, image = meet(values, sent)
    before, moved, newer, values, *sent = call(
        second_kernel,
        (shape(LOADS, LANES), VECTOR, VECTOR, VECTOR, *SENT),
        [SMEM] + [VMEM] * 11,
        [PICKS], 1 << 30, small, "second",
    )(where, table, *sums, inverse, modes, dual, image, multipliers, projected)
    sums, paired = meet(values, sent)
    multipliers, projected = call(
        last_kernel,
        (shape(SLOTS, LOADS),) * 2,
        [VMEM] * 12,
        [], 1 << 30, small, "last",
    )(*sums, before, inverse, modes, paired, image, moved, projected, newer)
    return (multipliers[None], projected[None])


def solution(mesh):
    return jax.shard_map(
        local,
        mesh=mesh,
        in_specs=(
            P(("cluster", "sub"), None, None, None),
            P(("cluster", "sub"), None, None),
            P(("cluster", "sub"), None, None),
            P(),
            P(("cluster", "sub"), None, None),
            P(("cluster", "sub"), None),
        ),
        out_specs=(P(("cluster", "sub"), None, None), P(("cluster", "sub"), None, None)),
        check_vma=False,
    )
```

```python
import functools

import jax
import jax.numpy as jnp
from jax import lax
from jax.experimental import pallas as pl
from jax.experimental.pallas import tpu as pltpu
from jax.sharding import PartitionSpec as P

F32 = jnp.float32
BF16 = jnp.bfloat16
HIGH = lax.Precision.HIGHEST

UNKNOWNS = 3072
SLOTS = 640
LOADS = 32
RHS = SLOTS + LOADS
TILE = 128
TILE_ROWS = 24
BLOCK = 256
BLOCKS = UNKNOWNS // BLOCK
SUBS = 32
CLUSTERS = 4
MODES = 6
LANES = 128
COARSE_AT = 96
OFFSETS = [
    (dz, dx, dy)
    for dz in (0, 1)
    for dx in (-1, 0, 1)
    for dy in (-1, 0, 1)
    if (dz, dx, dy) != (0, 0, 0)
]
PEERS = len(OFFSETS) + 2
SMALL = 1 << 22
CHUNK = 12
CHUNKS = 25
STEP = 128
GROUP = 4
VMEM = pl.BlockSpec(memory_space=pltpu.VMEM)
SMEM = pl.BlockSpec(memory_space=pltpu.SMEM)
ANY = pl.BlockSpec(memory_space=pl.ANY)


def nt(a, b, precision=None):
    return lax.dot_general(
        a, b, (((1,), (1,)), ((), ())), precision=precision, preferred_element_type=F32
    )


def nn(a, b, precision=None):
    return lax.dot_general(
        a, b, (((1,), (0,)), ((), ())), precision=precision, preferred_element_type=F32
    )


def halves(a):
    high = a.astype(BF16)
    return high, (a - high.astype(F32)).astype(BF16)


def thirds(a):
    high = a.astype(BF16)
    rest = a - high.astype(F32)
    middle = rest.astype(BF16)
    return jnp.concatenate([high, middle, (rest - middle.astype(F32)).astype(BF16)], axis=0)


def fold(a, rows):
    return a[:rows] + a[rows : 2 * rows] + a[2 * rows :]


def left3(a):
    high, low = halves(a)
    return jnp.concatenate([high, low, high], axis=1)


def right3(b):
    high, low = halves(b)
    return jnp.concatenate([high, high, low], axis=0)


def peers_of(me):
    z, x, y = me // 16, (me // 4) % 4, me % 4
    found = []
    for dz, dx, dy in OFFSETS:
        to_z = 1 - z if dz else z
        to_x, to_y = x + dx, y + dy
        valid = (to_x >= 0) & (to_x < 4) & (to_y >= 0) & (to_y < 4)
        found.append((valid, jnp.where(valid, to_z * 16 + to_x * 4 + to_y, me)))
    return found


def pick(picks, place, wanted):
    slot = lax.broadcasted_iota(jnp.int32, (SLOTS, LANES), 0)
    at = pl.ds(pl.multiple_of(place * LANES, LANES), LANES)
    picks[:, at] = jnp.where(slot == wanted, 1.0, 0.0).astype(BF16)


def select_slots(table, picks):
    def one(place, carry):
        at = pl.ds(pl.multiple_of(place * LANES, LANES), LANES)
        pick(picks, place, table[:1, at])
        return carry

    lax.fori_loop(0, PEERS, one, 0)


def send_values(values, extra, me, picks, to_sub, to_lower, to_upper):
    for peer in range(SUBS):
        to_sub[peer] = extra
    picked = fold(nn(thirds(values), picks[...]), values.shape[0])
    for place, (valid, peer) in enumerate(peers_of(me)):

        @pl.when(valid)
        def _():
            to_sub[peer] = picked[:, place * LANES : (place + 1) * LANES] + extra

    to_lower[...] = picked[:, (PEERS - 2) * LANES : (PEERS - 1) * LANES]
    to_upper[...] = picked[:, (PEERS - 1) * LANES :]


def received_sum(me, picks, sub, lower, upper):
    pieces = [sub[peer] for _, peer in peers_of(me)] + [lower[...], upper[...]]
    return fold(nt(thirds(jnp.concatenate(pieces, axis=1)), picks[...]), lower.shape[0])


def prepare_kernel(
    where, peer_slots, unknown_row, rigid,
    table, sorted_unknown, signs, ranks, counts, half, to_sub, to_lower, to_upper,
    peer_table, picks,
):
    me, cluster = where[0], where[1]
    found = peers_of(me)
    devices = peer_slots.shape[1]
    listed = jnp.concatenate(
        [
            peer_slots[...].astype(F32),
            jnp.full((LANES - peer_slots.shape[0], devices), float(SLOTS), F32),
        ],
        axis=0,
    )
    peer_table[...] = jnp.transpose(listed).astype(jnp.int32)
    base = cluster * SUBS
    own = base + me
    rows = [(valid, base + peer) for valid, peer in found]
    rows += [(own >= SUBS, jnp.maximum(own - SUBS, 0))]
    rows += [(own + SUBS < devices, jnp.minimum(own + SUBS, devices - 1))]
    for place, (valid, row) in enumerate(rows):
        pick(picks, place, jnp.where(valid, peer_table[pl.ds(row, 1), :], SLOTS))
    across = lax.broadcasted_iota(jnp.int32, (1, SLOTS), 1)
    key_row = unknown_row[...] * 1024 + across
    key_column = jnp.transpose(jnp.broadcast_to(key_row.astype(F32), (8, SLOTS)))[:, :1]
    key_column = key_column.astype(jnp.int32)
    rank = jnp.sum(jnp.where(key_column < key_row, 1.0, 0.0), axis=0, keepdims=True)
    rank_int = rank.astype(jnp.int32)
    ranks[...] = rank_int
    row = lax.broadcasted_iota(jnp.int32, (8, SLOTS), 0)
    coarse_rank = jnp.right_shift(rank_int, 8)
    digits = jnp.where(row == 0, coarse_rank, jnp.where(row == 1, rank_int - coarse_rank * 256, 1))
    moved = nn(digits.astype(F32).astype(BF16), picks[...])
    moved = moved[:1] * 256.0 + moved[1:2] + (1.0 - moved[2:3]) * 1024.0
    table[...] = jnp.broadcast_to(moved.astype(jnp.int32), (8, PEERS * LANES))
    ups = [jnp.where(peer > me, 1.0, -1.0) for _, peer in found] + [-1.0, 1.0]
    ups = jnp.concatenate([jnp.full((8, LANES), up, F32) for up in ups], axis=1)
    sign_row = nt(ups.astype(BF16), picks[...])[:1]
    unknown_float = unknown_row[...].astype(F32)
    for start in range(0, SLOTS, LANES):
        match = lax.broadcasted_iota(jnp.int32, (LANES, SLOTS), 0) + start == rank_int
        at = slice(start, start + LANES)
        sorted_unknown[at] = jnp.sum(
            jnp.where(match, unknown_float, 0.0), axis=1, keepdims=True
        ).astype(jnp.int32)
        signs[at] = jnp.sum(jnp.where(match, sign_row, 0.0), axis=1, keepdims=True)
    for block in range(BLOCKS):
        within = jnp.where(unknown_row[...] < (block + 1) * BLOCK, 1.0, 0.0)
        counts[block] = (jnp.sum(within).astype(jnp.int32) + STEP - 1) // STEP
    select_slots(table, picks)
    own = jnp.zeros((24, SLOTS), F32)
    lane = lax.broadcasted_iota(jnp.int32, (SLOTS, BLOCK), 1)
    for block in range(BLOCKS):
        rows = [rigid[mode, :, block * BLOCK : (block + 1) * BLOCK] for mode in range(MODES)]
        rows = jnp.concatenate(rows + [jnp.zeros((8 - MODES, BLOCK), F32)], axis=0)
        glue = jnp.where(sorted_unknown[...] - block * BLOCK == lane, signs[...], 0.0).astype(BF16)
        own = own + nt(thirds(rows), glue)
    own = fold(own, 8)
    row = lax.broadcasted_iota(jnp.int32, (LOADS, SLOTS), 0)
    placed = jnp.zeros((LOADS, SLOTS), F32)
    for mode in range(MODES):
        placed = jnp.where(row == cluster * MODES + mode, own[mode : mode + 1, :], placed)
    half[...] = placed
    send_values(placed, jnp.zeros((LOADS, LANES), F32), me, picks, to_sub, to_lower, to_upper)


def invert_diagonal(diag, beside, inverse, high, low):
    base, group, some = 32, 8, 12
    lane = lax.broadcasted_iota(jnp.int32, (some, group, TILE), 2)
    row = lax.broadcasted_iota(jnp.int32, (some, group, TILE), 1)
    flat_lane = lax.broadcasted_iota(jnp.int32, (some * group, TILE), 1)
    for start in range(0, TILE_ROWS, some):
        tiles = slice(start, start + some)
        given, solved = [], []
        for g in range(base // group):
            block = jnp.zeros((some, group, TILE), F32)
            for b in range(TILE // base):
                at = b * base + g * group
                block = jnp.where(lane // base == b, diag[tiles, at : at + group, :], block)
            given.append(block.reshape(some * group, TILE))
            solved.append(jnp.where(row + g * group == lane % base, 1.0, 0.0))
        for k in range(base):
            now, at = k // group, k % group
            column = [None] * (base // group)
            for g in range(now, base // group):
                column[g] = jnp.take_along_axis(
                    given[g], flat_lane // base * base + k, axis=1, mode="promise_in_bounds"
                ).reshape(some, group, TILE)
            pivot = solved[now][:, at : at + 1, :] / column[now][:, at : at + 1, :]
            solved[now] = jnp.where(
                row == at,
                pivot,
                jnp.where(row > at, solved[now] - column[now] * pivot, solved[now]),
            )
            for g in range(now + 1, base // group):
                solved[g] = solved[g] - column[g] * pivot
        for g in range(base // group):
            for b in range(TILE // base):
                at = b * base + g * group
                inverse[tiles, at : at + group, :] = jnp.where(lane // base == b, solved[g], 0.0)
    half, quarter = TILE // 2, TILE // 4
    lane = lax.broadcasted_iota(jnp.int32, (quarter, TILE), 1)
    none = jnp.zeros((quarter, TILE), F32)
    for t in range(TILE_ROWS):
        odd = [slice(quarter, half), slice(half + quarter, TILE)]
        below = [
            jnp.where(lane < quarter, diag[t, odd[0], :], 0.0),
            jnp.where((lane >= half) & (lane < half + quarter), diag[t, odd[1], :], 0.0),
        ]
        partial = nn(left3(jnp.concatenate(below, axis=0)), right3(inverse[t]))
        partial = jnp.concatenate([none, partial[:quarter], none, partial[quarter:]], axis=0)
        rows = jnp.concatenate([inverse[t, odd[0], :], inverse[t, odd[1], :]], axis=0)
        rows = rows - nn(left3(rows), right3(partial))
        inverse[t, odd[0], :] = rows[:quarter]
        inverse[t, odd[1], :] = rows[quarter:]
    lane = lax.broadcasted_iota(jnp.int32, (half, TILE), 1)
    for t in range(TILE_ROWS):
        below = jnp.where(lane < half, diag[t, half:, :], 0.0)
        partial = nn(left3(below), right3(inverse[t]))
        partial = jnp.concatenate([jnp.zeros((half, TILE), F32), partial], axis=0)
        rows = inverse[t, half:, :]
        inverse[t, half:, :] = rows - nn(left3(rows), right3(partial))
    for j in range(BLOCKS):
        first, second = inverse[2 * j], inverse[2 * j + 1]
        off = -nn(left3(second), right3(nn(left3(beside[j]), right3(first))))
        whole = jnp.concatenate(
            [
                jnp.concatenate([first, jnp.zeros((TILE, TILE), F32)], axis=1),
                jnp.concatenate([off, second], axis=1),
            ],
            axis=0,
        )
        high[j], low[j] = halves(whole)


def solve_kernel(
    counts, tiles, unknown, signs, loads, dual, load,
    held, xh, xl, total, diag, beside, inverse, high, low, sems, early_sems,
):
    def copy(c):
        at = pl.ds(c * CHUNK, CHUNK)
        return pltpu.make_async_copy(tiles.at[at], held.at[at], sems.at[c])

    early = []
    for t in range(TILE_ROWS):
        at = t * (t + 1) // 2 + t
        early.append(pltpu.make_async_copy(tiles.at[at], diag.at[t], early_sems.at[t]))
        if t % 2:
            early.append(
                pltpu.make_async_copy(
                    tiles.at[at - 1], beside.at[t // 2], early_sems.at[TILE_ROWS + t // 2]
                )
            )
    for one in early:
        one.start()
    for c in range(CHUNKS):
        copy(c).start()
    dual[...] = jnp.zeros_like(dual)
    load[...] = jnp.zeros_like(load)
    lane = lax.broadcasted_iota(jnp.int32, (SLOTS, BLOCK), 1)
    for i in range(BLOCKS):
        total[i, :LOADS] = loads[:, i * BLOCK : (i + 1) * BLOCK]
        total[i, LOADS:] = jnp.where(unknown[...] - i * BLOCK == lane, signs[...], 0.0)
    for one in early:
        one.wait()
    invert_diagonal(diag, beside, inverse, high, low)
    for c in range(CHUNKS):
        copy(c).wait()

    def block_column(k, carry):
        right = jnp.concatenate([high[k], high[k], low[k]], axis=1)
        for c in range(SLOTS // STEP + 1):

            @pl.when(counts[k] == c)
            def _():
                m = LOADS + c * STEP
                ah, al = halves(total[k, :m])
                solved = nt(jnp.concatenate([ah, al, ah], axis=1), right)
                ah, al = halves(solved)
                xh[:m], xl[:m] = ah, al
                if c:
                    product = nt(
                        jnp.concatenate([ah, al, ah], axis=1),
                        jnp.concatenate([ah[LOADS:], ah[LOADS:], al[LOADS:]], axis=1),
                    )
                    load[:, : c * STEP] += product[:LOADS]
                    dual[: c * STEP, : c * STEP] += product[LOADS:]

                def update(group, carry):
                    left = jnp.concatenate([xh[:m], xl[:m], xh[:m]], axis=1)
                    for j in range(GROUP):
                        i = BLOCKS - 1 - j - group * GROUP
                        upper = i * (2 * i + 1) + 2 * k
                        under = upper + 2 * i + 1
                        tile = jnp.concatenate(
                            [
                                jnp.concatenate([held[upper], held[upper + 1]], axis=1),
                                jnp.concatenate([held[under], held[under + 1]], axis=1),
                            ],
                            axis=0,
                        )
                        th, tl = halves(tile)
                        total[i, :m] -= nt(left, jnp.concatenate([th, th, tl], axis=1))
                    return carry

                lax.fori_loop(0, (BLOCKS - 1 - k + GROUP - 1) // GROUP, update, 0)

        return carry

    lax.fori_loop(0, BLOCKS, block_column, 0)


def pack_gram(gram, extra):
    lane = lax.broadcasted_iota(jnp.int32, extra.shape, 1)
    gram = coarse_lanes(gram)
    columns = jnp.concatenate([pltpu.roll(gram, 24, 1), pltpu.roll(gram, 16, 1)], axis=0)
    rows = jnp.concatenate([jnp.zeros((56, LANES), F32), gram[16:24]], axis=0)
    return jnp.where(lane >= COARSE_AT + CLUSTERS * MODES, columns, coarse_lanes(extra) + rows)


def unpack_gram(sums):
    row = lax.broadcasted_iota(jnp.int32, (LOADS, LANES), 0)
    lane = lax.broadcasted_iota(jnp.int32, (LOADS, LANES), 1)
    known = jnp.where(lane < 8, pltpu.roll(sums[:LOADS], 8, 1), pltpu.roll(sums[LOADS:], 16, 1))
    rows = pltpu.roll(sums[56:], 32, 1)
    rows = jnp.concatenate([jnp.zeros((16, LANES), F32), rows, jnp.zeros((8, LANES), F32)], axis=0)
    known = jnp.where(lane < 16, known, jnp.where((row >= 16) & (row < 24), rows, 0.0))
    known = jnp.where((lane < 24) & (row < 24), known, 0.0)
    turned = nt(jnp.where(row == lane, 1.0, 0.0), known, HIGH)
    turned = jnp.concatenate([turned, jnp.zeros((LOADS, LANES - LOADS), F32)], axis=1)
    return jnp.where((row < 16) & (lane >= 16), turned, known)


def gram_inverse(filled):
    row = lax.broadcasted_iota(jnp.int32, (LOADS, LANES), 0)
    lane = lax.broadcasted_iota(jnp.int32, (LOADS, LANES), 1)
    filled = jnp.where((row >= CLUSTERS * MODES) & (row == lane), 1.0, filled)
    filled = jnp.where(lane == row + LOADS, 1.0, filled)
    for k in range(CLUSTERS * MODES):
        pivot = filled[k : k + 1, :] / filled[k : k + 1, k : k + 1]
        factor = jnp.where(row[:, :1] > k, filled[:, k : k + 1], 0.0)
        filled = filled - factor * pivot
    scale = jnp.sum(jnp.where(row == lane, filled, 0.0), axis=1, keepdims=True)
    lower = jnp.where((lane >= LOADS) & (lane < 2 * LOADS) & (row < CLUSTERS * MODES), filled, 0.0)
    lower = lower * lax.rsqrt(scale)
    lower = pltpu.roll(lower, COARSE_AT - LOADS, 1)
    return lax.dot_general(
        lower, lower, (((0,), (0,)), ((), ())), precision=HIGH, preferred_element_type=F32
    )


def coarse_lanes(values):
    lane = lax.broadcasted_iota(jnp.int32, values.shape, 1)
    return jnp.where((lane >= COARSE_AT) & (lane < COARSE_AT + CLUSTERS * MODES), values, 0.0)


def with_scalars(values, *scalars):
    lane = lax.broadcasted_iota(jnp.int32, values.shape, 1)
    values = coarse_lanes(values)
    for place, scalar in enumerate(scalars):
        values = jnp.where(lane == COARSE_AT + CLUSTERS * MODES + place, scalar, values)
    return values


def scalar(values, place):
    at = COARSE_AT + CLUSTERS * MODES + place
    return values[:, at : at + 1]


def rows_sum(a, b):
    return jnp.sum(a * b, axis=1, keepdims=True)


def start_kernel(
    where, table, half, sub, lower, upper, dual, load,
    modes, values, to_sub, to_lower, to_upper, picks,
):
    select_slots(table, picks)
    total = half[...] + received_sum(where[0], picks, sub, lower, upper)
    modes[...] = jnp.concatenate([jnp.zeros((COARSE_AT, SLOTS), F32), total], axis=0)
    values[:LOADS] = load[...]
    values[LOADS:] = nn(total, dual[...], HIGH)
    extra = nt(values[...], modes[...], HIGH)
    extra = pack_gram(0.5 * nt(total, modes[...], HIGH), extra)
    send_values(values[...], extra, where[0], picks, to_sub, to_lower, to_upper)


def pair_kernel(where, table, values, sub, lower, upper, paired, picks):
    select_slots(table, picks)
    paired[...] = values[...] + received_sum(where[0], picks, sub, lower, upper)


def first_kernel(
    where, table, s0, s1, s2, s3, coarse_load, modes, dual, paired,
    inverse, multipliers, projected, values, to_sub, to_lower, to_upper, picks,
):
    select_slots(table, picks)
    sums = (s0[...] + s1[...]) + (s2[...] + s3[...])
    inverse[...] = gram_inverse(unpack_gram(sums))
    begin = nn(coarse_load[...], inverse[...], HIGH)
    multipliers[...] = nn(begin, modes[...], HIGH)
    images = jnp.concatenate([jnp.zeros((COARSE_AT, SLOTS), F32), paired[LOADS:]], axis=0)
    residual = paired[:LOADS] - nn(begin, images, HIGH)
    sums = coarse_lanes(sums)
    curved = jnp.concatenate([jnp.zeros((COARSE_AT, LANES), F32), sums[LOADS:]], axis=0)
    weights = nn(sums[:LOADS] - nn(begin, curved, HIGH), inverse[...], HIGH)
    projected[...] = residual - nn(weights, modes[...], HIGH)
    values[...] = nn(projected[...], dual[...], HIGH)
    extra = with_scalars(
        nt(values[...], modes[...], HIGH),
        0.5 * rows_sum(projected[...], projected[...]),
        rows_sum(projected[...], values[...]),
    )
    send_values(values[...], extra, where[0], picks, to_sub, to_lower, to_upper)


def second_kernel(
    where, table, s0, s1, s2, s3, inverse, modes, dual, image, multipliers, projected,
    sums, moved, newer, values, to_sub, to_lower, to_upper, picks,
):
    select_slots(table, picks)
    sums[...] = (s0[...] + s1[...]) + (s2[...] + s3[...])
    alpha = scalar(sums, 0) / scalar(sums, 1)
    weights = nn(coarse_lanes(sums[...]), inverse[...], HIGH)
    moved[...] = multipliers[...] + alpha * projected[...]
    newer[...] = projected[...] - alpha * (image[...] - nn(weights, modes[...], HIGH))
    values[...] = nn(newer[...], dual[...], HIGH)
    extra = with_scalars(
        nt(values[...], modes[...], HIGH),
        0.5 * rows_sum(newer[...], newer[...]),
        rows_sum(newer[...], values[...]),
        0.5 * rows_sum(newer[...], image[...]),
    )
    send_values(values[...], extra, where[0], picks, to_sub, to_lower, to_upper)


def last_kernel(
    s0, s1, s2, s3, before, inverse, modes, paired, image, moved, projected, newer, ranks,
    multipliers_out, projected_out,
):
    sums = (s0[...] + s1[...]) + (s2[...] + s3[...])
    following = scalar(sums, 0)
    beta = following / scalar(before, 0)
    curvature = scalar(sums, 1) + beta * (2.0 * scalar(sums, 2) + beta * scalar(before, 1))
    alpha = following / curvature
    direction = newer[...] + beta * projected[...]
    image_now = paired[...] + beta * image[...]
    coarse = coarse_lanes(sums + beta * before[...])
    weights = nn(coarse, inverse[...], HIGH)
    both = jnp.concatenate(
        [
            moved[...] + alpha * direction,
            newer[...] - alpha * (image_now - nn(weights, modes[...], HIGH)),
        ],
        axis=0,
    )
    back = lax.broadcasted_iota(jnp.int32, (SLOTS, SLOTS), 0) == ranks[...]
    both = fold(nn(thirds(both), jnp.where(back, 1.0, 0.0).astype(BF16)), 2 * LOADS)
    multipliers_out[...] = both[:LOADS]
    projected_out[...] = both[LOADS:]


def shape(*dims, dtype=F32):
    return jax.ShapeDtypeStruct(dims, dtype)


def sent_shapes(rows):
    return (shape(SUBS, rows, LANES), shape(rows, LANES), shape(rows, LANES))


SENT = sent_shapes(LOADS)
VECTOR = shape(LOADS, SLOTS)
PICKS = pltpu.VMEM((SLOTS, PEERS * LANES), BF16)


def call(
    kernel, out_shape, in_specs, scratch, flops, moved, name, limit=24, out_specs=None
):
    return pl.pallas_call(
        kernel,
        out_shape=out_shape,
        in_specs=in_specs,
        out_specs=out_specs or jax.tree.map(lambda _: VMEM, out_shape),
        scratch_shapes=scratch,
        cost_estimate=pl.CostEstimate(flops=flops, bytes_accessed=moved, transcendentals=0),
        compiler_params=pltpu.CompilerParams(vmem_limit_bytes=limit << 20),
        name=name,
    )


def run_solve(counts, tiles, unknown, signs, loads):
    return call(
        solve_kernel,
        (shape(SLOTS, SLOTS), VECTOR),
        [SMEM, ANY] + [VMEM] * 3,
        [
            pltpu.VMEM(tiles.shape, F32),
            pltpu.VMEM((RHS, BLOCK), BF16),
            pltpu.VMEM((RHS, BLOCK), BF16),
            pltpu.VMEM((BLOCKS, RHS, BLOCK), F32),
            pltpu.VMEM((TILE_ROWS, TILE, TILE), F32),
            pltpu.VMEM((BLOCKS, TILE, TILE), F32),
            pltpu.VMEM((TILE_ROWS, TILE, TILE), F32),
            pltpu.VMEM((BLOCKS, BLOCK, BLOCK), BF16),
            pltpu.VMEM((BLOCKS, BLOCK, BLOCK), BF16),
            pltpu.SemaphoreType.DMA((CHUNKS,)),
            pltpu.SemaphoreType.DMA((TILE_ROWS + BLOCKS,)),
        ],
        30 << 30, 5 * SMALL, "solve", 50,
    )(counts, tiles, unknown, signs, loads)


def exchange(sent):
    to_sub, to_lower, to_upper = sent
    up = [(c, c + 1) for c in range(CLUSTERS - 1)]
    down = [(c + 1, c) for c in range(CLUSTERS - 1)]
    from_lower = lax.ppermute(to_upper, "cluster", up)
    from_upper = lax.ppermute(to_lower, "cluster", down)
    received = lax.all_to_all(to_sub, "sub", split_axis=0, concat_axis=0, tiled=True)
    return received, from_lower, from_upper


def cluster_sums(received):
    own = jnp.sum(received, axis=0)
    others = [
        lax.ppermute(own, "cluster", [(c, (c + by) % CLUSTERS) for c in range(CLUSTERS)])
        for by in (1, 2, 3)
    ]
    return (own, *others)


def local(factor_tiles, rigid_modes, load_cases, coarse_load, peer_slots, slot_unknown):
    cluster = lax.axis_index("cluster")
    me = lax.axis_index("sub")
    where = jnp.stack([me, cluster]).astype(jnp.int32)

    table, unknown, signs, ranks, counts, half, *sent = call(
        prepare_kernel,
        (
            shape(8, PEERS * LANES, dtype=jnp.int32),
            shape(SLOTS, 1, dtype=jnp.int32),
            shape(SLOTS, 1),
            shape(1, SLOTS, dtype=jnp.int32),
            shape(16, dtype=jnp.int32),
            VECTOR,
            *SENT,
        ),
        [SMEM, VMEM, VMEM, VMEM],
        [pltpu.VMEM((CLUSTERS * SUBS, LANES), jnp.int32), PICKS],
        1 << 30, SMALL, "prepare",
        out_specs=(VMEM, VMEM, VMEM, VMEM, SMEM, VMEM, VMEM, VMEM, VMEM),
    )(where, peer_slots[0].T, slot_unknown, jnp.swapaxes(rigid_modes, 0, 1))
    received = exchange(sent)
    dual, load = run_solve(counts, factor_tiles[0], unknown, signs, load_cases[0])

    modes, values, *sent = call(
        start_kernel,
        (shape(LANES, SLOTS), shape(2 * LOADS, SLOTS), *sent_shapes(2 * LOADS)),
        [SMEM] + [VMEM] * 7,
        [PICKS], 1 << 30, SMALL, "start",
    )(where, table, half, *received, dual, load)

    def meet(values, sent):
        received = exchange(sent)
        sums = cluster_sums(received[0])
        paired = call(
            pair_kernel,
            shape(*values.shape),
            [SMEM] + [VMEM] * 5,
            [PICKS], 1 << 30, SMALL, "pair",
        )(where, table, values, *received)
        return sums, paired

    sums, paired = meet(values, sent)
    spread_load = jnp.pad(
        coarse_load.T, ((0, 0), (COARSE_AT, LANES - COARSE_AT - CLUSTERS * MODES))
    )
    inverse, multipliers, projected, values, *sent = call(
        first_kernel,
        (shape(LANES, LANES), VECTOR, VECTOR, VECTOR, *SENT),
        [SMEM] + [VMEM] * 9,
        [PICKS], 1 << 30, SMALL, "first",
    )(where, table, *sums, spread_load, modes, dual, paired)
    sums, image = meet(values, sent)
    before, moved, newer, values, *sent = call(
        second_kernel,
        (shape(LOADS, LANES), VECTOR, VECTOR, VECTOR, *SENT),
        [SMEM] + [VMEM] * 11,
        [PICKS], 1 << 30, SMALL, "second",
    )(where, table, *sums, inverse, modes, dual, image, multipliers, projected)
    sums, paired = meet(values, sent)
    multipliers, projected = call(
        last_kernel,
        (VECTOR, VECTOR),
        [VMEM] * 13,
        [], 1 << 30, SMALL, "last",
    )(*sums, before, inverse, modes, paired, image, moved, projected, newer, ranks)
    return (multipliers.T[None], projected.T[None])


def solution(mesh):
    return jax.shard_map(
        local,
        mesh=mesh,
        in_specs=(
            P(("cluster", "sub"), None, None, None),
            P(("cluster", "sub"), None, None),
            P(("cluster", "sub"), None, None),
            P(),
            P(("cluster", "sub"), None, None),
            P(("cluster", "sub"), None),
        ),
        out_specs=(P(("cluster", "sub"), None, None), P(("cluster", "sub"), None, None)),
        check_vma=False,
    )
```

```python
import functools

import jax
import jax.numpy as jnp
from jax import lax
from jax.experimental import pallas as pl
from jax.experimental.pallas import tpu as pltpu
from jax.sharding import PartitionSpec as P

F32 = jnp.float32
BF16 = jnp.bfloat16
HIGH = lax.Precision.HIGHEST

UNKNOWNS = 3072
SLOTS = 640
LOADS = 32
RHS = SLOTS + LOADS
TILE = 128
TILE_ROWS = 24
BLOCK = 256
BLOCKS = UNKNOWNS // BLOCK
SUBS = 32
CLUSTERS = 4
MODES = 6
COARSE = CLUSTERS * MODES
ROWS = LOADS + COARSE
LANES = 128
COARSE_AT = 96
FACES = [(0, 0, 1), (0, 0, -1), (0, 1, 0), (0, -1, 0), (1, 0, 0)]
EDGES = [(0, 1, 1), (0, 1, -1), (1, 0, 1), (1, 1, 0), (1, 1, 1), (1, 1, -1)]
SLOT, EDGE_MOST = 16, 12
LOWER, UPPER, EDGE = len(FACES), len(FACES) + 1, len(FACES) + 2
PLACES = len(FACES) + 4
SMALL = 1 << 22
CHUNK = 12
CHUNKS = 25
STEP = 128
GROUP = 4
VMEM = pl.BlockSpec(memory_space=pltpu.VMEM)
SMEM = pl.BlockSpec(memory_space=pltpu.SMEM)
ANY = pl.BlockSpec(memory_space=pl.ANY)


def nt(a, b, precision=None):
    return lax.dot_general(
        a, b, (((1,), (1,)), ((), ())), precision=precision, preferred_element_type=F32
    )


def nn(a, b, precision=None):
    return lax.dot_general(
        a, b, (((1,), (0,)), ((), ())), precision=precision, preferred_element_type=F32
    )


def halves(a):
    high = a.astype(BF16)
    return high, (a - high.astype(F32)).astype(BF16)


def thirds(a):
    high = a.astype(BF16).astype(F32)
    rest = a - high
    middle = rest.astype(BF16).astype(F32)
    return jnp.concatenate([high, middle, rest - middle], axis=0).astype(BF16)


def fold(a, rows):
    return a[:rows] + a[rows : 2 * rows] + a[2 * rows :]


def times(dot, high, low, right_high, right_low):
    m = high.shape[0]
    product = dot(jnp.concatenate([high, low], axis=0), right_high)
    return product[:m] + product[m:] + dot(high, right_low)


def mm(a, b):
    return times(nn, *halves(a), *halves(b))


def opposite(offset):
    return (offset[0], -offset[1], -offset[2])


def peer_of(me, offset):
    dz, dx, dy = offset
    z, x, y = me // 16, (me // 4) % 4 + dx, me % 4 + dy
    valid = (x >= 0) & (x < 4) & (y >= 0) & (y < 4)
    return valid, jnp.where(valid, (1 - z if dz else z) * 16 + x * 4 + y, me)


def edges():
    for side in (0, 1):
        for slot, offset in enumerate(EDGES):
            yield side, slot, opposite(offset) if side else offset


def in_slot(shape, slot):
    lane = lax.broadcasted_iota(jnp.int32, shape, 1)
    return (lane >= slot * SLOT) & (lane < slot * SLOT + EDGE_MOST)


def lanes_of(values, place):
    return values[:, place * LANES : (place + 1) * LANES]


def pick(picks, place, wanted):
    slot = lax.broadcasted_iota(jnp.int32, (SLOTS, LANES), 0)
    at = pl.ds(pl.multiple_of(place * LANES, LANES), LANES)
    picks[:, at] = jnp.where(slot == wanted, 1.0, 0.0).astype(BF16)


def select_slots(table, picks):
    def one(place, carry):
        at = pl.ds(pl.multiple_of(place * LANES, LANES), LANES)
        pick(picks, place, table[:1, at])
        return carry

    lax.fori_loop(0, PLACES, one, 0)


def send_values(values, extra, me, picks, to_sub, to_lower, to_upper):
    rows = values.shape[0]
    for peer in range(SUBS):
        to_sub[peer] = extra
    picked = fold(nn(thirds(values), picks[...]), rows)
    for place, offset in enumerate(FACES):
        valid, peer = peer_of(me, offset)

        @pl.when(valid)
        def _():
            to_sub[peer] = lanes_of(picked, place) + extra

    for side, slot, offset in edges():
        valid, peer = peer_of(me, offset)

        @pl.when(valid)
        def _():
            mine = lanes_of(picked, EDGE + side)
            to_sub[peer] = jnp.where(in_slot(mine.shape, slot), mine, extra)

    to_lower[...] = lanes_of(picked, LOWER)
    to_upper[...] = lanes_of(picked, UPPER)


def edge_blocks(me, sub, rows):
    blocks = [jnp.zeros((rows, LANES), F32)] * 2
    for side, slot, offset in edges():
        came = sub[peer_of(me, offset)[1]][:rows]
        blocks[side] = jnp.where(in_slot((rows, LANES), slot), came, blocks[side])
    return blocks


def received_sum(me, picks, sub, lower, upper):
    rows = lower.shape[0]
    pieces = [sub[peer_of(me, offset)[1]] for offset in FACES]
    pieces += [lower[...], upper[...]] + edge_blocks(me, sub, rows)
    return fold(nt(thirds(jnp.concatenate(pieces, axis=1)), picks[...]), rows)


def by_cluster(cluster, parts):
    row = lax.broadcasted_iota(jnp.int32, (LOADS, SLOTS), 0)
    placed = jnp.zeros((LOADS, SLOTS), F32)
    for step, part in parts:
        for mode in range(MODES):
            at = (cluster + step) * MODES + mode
            placed = placed + jnp.where(row == at, part[mode : mode + 1, :], 0.0)
    return placed


def prepare_kernel(
    where, peer_slots, unknown_row, rigid,
    table, sorted_unknown, signs, ranks, counts, half, to_sub, to_lower, to_upper,
    peer_table, picks,
):
    me, cluster = where[0], where[1]
    devices = peer_slots.shape[1]
    listed = jnp.concatenate(
        [
            peer_slots[...].astype(F32),
            jnp.full((LANES - peer_slots.shape[0], devices), float(SLOTS), F32),
        ],
        axis=0,
    )
    peer_table[...] = jnp.transpose(listed).astype(jnp.int32)
    base = cluster * SUBS
    own = base + me

    def wanted_of(valid, row):
        return jnp.where(valid, peer_table[pl.ds(row, 1), :], SLOTS)

    ups = []
    for place, offset in enumerate(FACES):
        valid, peer = peer_of(me, offset)
        pick(picks, place, wanted_of(valid, base + peer))
        ups.append(jnp.full((8, LANES), jnp.where(peer > me, 1.0, -1.0), F32))
    pick(picks, LOWER, wanted_of(own >= SUBS, jnp.maximum(own - SUBS, 0)))
    pick(picks, UPPER, wanted_of(own + SUBS < devices, jnp.minimum(own + SUBS, devices - 1)))
    ups += [jnp.full((8, LANES), -1.0, F32), jnp.full((8, LANES), 1.0, F32)]
    wanted = [jnp.full((1, LANES), SLOTS, jnp.int32)] * 2
    signs_of = [jnp.full((8, LANES), 1.0, F32)] * 2
    for side, slot, offset in edges():
        valid, peer = peer_of(me, offset)
        row = wanted_of(valid, base + peer)
        row = pltpu.roll(row, slot * SLOT, 1) if slot else row
        wanted[side] = jnp.where(in_slot((1, LANES), slot), row, wanted[side])
        signs_of[side] = jnp.where(
            in_slot((8, LANES), slot), jnp.where(peer > me, 1.0, -1.0), signs_of[side]
        )
    pick(picks, EDGE, wanted[0])
    pick(picks, EDGE + 1, wanted[1])
    ups = jnp.concatenate(ups + signs_of, axis=1)
    across = lax.broadcasted_iota(jnp.int32, (1, SLOTS), 1)
    key_row = unknown_row[...] * 1024 + across
    key_column = jnp.transpose(jnp.broadcast_to(key_row.astype(F32), (8, SLOTS)))[:, :1]
    key_column = key_column.astype(jnp.int32)
    rank = jnp.sum(jnp.where(key_column < key_row, 1.0, 0.0), axis=0, keepdims=True)
    rank_int = rank.astype(jnp.int32)
    ranks[...] = rank_int
    row = lax.broadcasted_iota(jnp.int32, (8, SLOTS), 0)
    coarse_rank = jnp.right_shift(rank_int, 8)
    digits = jnp.where(row == 0, coarse_rank, jnp.where(row == 1, rank_int - coarse_rank * 256, 1))
    moved = nn(digits.astype(F32).astype(BF16), picks[...])
    moved = moved[:1] * 256.0 + moved[1:2] + (1.0 - moved[2:3]) * 1024.0
    table[...] = jnp.broadcast_to(moved.astype(jnp.int32), (8, PLACES * LANES))
    sign_row = nt(ups.astype(BF16), picks[...])[:1]
    unknown_float = unknown_row[...].astype(F32)
    for start in range(0, SLOTS, LANES):
        match = lax.broadcasted_iota(jnp.int32, (LANES, SLOTS), 0) + start == rank_int
        at = slice(start, start + LANES)
        sorted_unknown[at] = jnp.sum(
            jnp.where(match, unknown_float, 0.0), axis=1, keepdims=True
        ).astype(jnp.int32)
        signs[at] = jnp.sum(jnp.where(match, sign_row, 0.0), axis=1, keepdims=True)
    for block in range(BLOCKS):
        within = jnp.where(unknown_row[...] < (block + 1) * BLOCK, 1.0, 0.0)
        counts[block] = (jnp.sum(within).astype(jnp.int32) + STEP - 1) // STEP
    select_slots(table, picks)
    own = jnp.zeros((24, SLOTS), F32)
    lane = lax.broadcasted_iota(jnp.int32, (SLOTS, BLOCK), 1)
    for block in range(BLOCKS):
        rows = [rigid[mode, :, block * BLOCK : (block + 1) * BLOCK] for mode in range(MODES)]
        rows = jnp.concatenate(rows + [jnp.zeros((8 - MODES, BLOCK), F32)], axis=0)
        glue = jnp.where(sorted_unknown[...] - block * BLOCK == lane, signs[...], 0.0).astype(BF16)
        own = own + nt(thirds(rows), glue)
    own = fold(own, 8)
    half[...] = own
    send_values(own, jnp.zeros((8, LANES), F32), me, picks, to_sub, to_lower, to_upper)


def invert_diagonal(diag, beside, inverse, high, low):
    base, group, some, many = 32, 8, 12, 12
    lane3 = lax.broadcasted_iota(jnp.int32, (some, group, TILE), 2)
    row = lax.broadcasted_iota(jnp.int32, (some, group, TILE), 1)
    flat_lane = lax.broadcasted_iota(jnp.int32, (some * group, TILE), 1)

    def substitute(step, carry):
        tiles = pl.ds(step * some, some)
        given, solved = [], []
        for g in range(base // group):
            block = jnp.zeros((some, group, TILE), F32)
            for b in range(TILE // base):
                at = b * base + g * group
                block = jnp.where(lane3 // base == b, diag[tiles, at : at + group, :], block)
            given.append(block.reshape(some * group, TILE))
            solved.append(jnp.where(row + g * group == lane3 % base, 1.0, 0.0))
        for k in range(base):
            now, at = k // group, k % group
            column = [None] * (base // group)
            for g in range(now, base // group):
                column[g] = jnp.take_along_axis(
                    given[g], flat_lane // base * base + k, axis=1, mode="promise_in_bounds"
                ).reshape(some, group, TILE)
            pivot = solved[now][:, at : at + 1, :] / column[now][:, at : at + 1, :]
            solved[now] = jnp.where(
                row == at,
                pivot,
                jnp.where(row > at, solved[now] - column[now] * pivot, solved[now]),
            )
            for g in range(now + 1, base // group):
                solved[g] = solved[g] - column[g] * pivot
        for g in range(base // group):
            for b in range(TILE // base):
                at = b * base + g * group
                inverse[tiles, at : at + group, :] = jnp.where(lane3 // base == b, solved[g], 0.0)
        return carry

    lax.fori_loop(0, TILE_ROWS // some, substitute, 0)
    half, quarter = TILE // 2, TILE // 4
    odd = [slice(quarter, half), slice(half + quarter, TILE)]
    lane = lax.broadcasted_iota(jnp.int32, (quarter, TILE), 1)
    none = jnp.zeros((quarter, TILE), F32)

    def merge_quarters(step, carry):
        for n in range(many):
            t = step * many + n
            below = [
                jnp.where(lane < quarter, diag[t, odd[0], :], 0.0),
                jnp.where((lane >= half) & (lane < half + quarter), diag[t, odd[1], :], 0.0),
            ]
            partial = mm(jnp.concatenate(below, axis=0), inverse[t])
            partial = jnp.concatenate([none, partial[:quarter], none, partial[quarter:]], axis=0)
            rows = jnp.concatenate([inverse[t, odd[0], :], inverse[t, odd[1], :]], axis=0)
            rows = rows - mm(rows, partial)
            inverse[t, odd[0], :] = rows[:quarter]
            inverse[t, odd[1], :] = rows[quarter:]
        return carry

    lax.fori_loop(0, TILE_ROWS // many, merge_quarters, 0)

    def merge_halves(step, carry):
        for n in range(many):
            t = step * many + n
            partial = mm(diag[t, half:, :half], inverse[t, :half, :half])
            inverse[t, half:, :half] = -mm(inverse[t, half:, half:], partial)
        return carry

    lax.fori_loop(0, TILE_ROWS // many, merge_halves, 0)

    def merge_tiles(step, carry):
        for n in range(many // 2):
            j = step * (many // 2) + n
            first, second = inverse[2 * j], inverse[2 * j + 1]
            off = -mm(second, mm(beside[j], first))
            whole = jnp.concatenate(
                [
                    jnp.concatenate([first, jnp.zeros((TILE, TILE), F32)], axis=1),
                    jnp.concatenate([off, second], axis=1),
                ],
                axis=0,
            )
            high[j], low[j] = halves(whole)
        return carry

    lax.fori_loop(0, 2 * BLOCKS // many, merge_tiles, 0)


def solve_kernel(
    counts, tiles, unknown, signs, loads, dual, load,
    held, xh, xl, total, diag, beside, inverse, high, low, sems, early_sems,
):
    def copy(c):
        at = pl.ds(c * CHUNK, CHUNK)
        return pltpu.make_async_copy(tiles.at[at], held.at[at], sems.at[c])

    early = []
    for t in range(TILE_ROWS):
        at = t * (t + 1) // 2 + t
        early.append(pltpu.make_async_copy(tiles.at[at], diag.at[t], early_sems.at[t]))
        if t % 2:
            early.append(
                pltpu.make_async_copy(
                    tiles.at[at - 1], beside.at[t // 2], early_sems.at[TILE_ROWS + t // 2]
                )
            )
    for one in early:
        one.start()
    for c in range(CHUNKS):
        copy(c).start()
    dual[...] = jnp.zeros_like(dual)
    load[...] = jnp.zeros_like(load)
    lane = lax.broadcasted_iota(jnp.int32, (SLOTS, BLOCK), 1)
    for i in range(BLOCKS):
        total[i, :LOADS] = loads[:, i * BLOCK : (i + 1) * BLOCK]
        total[i, LOADS:] = jnp.where(unknown[...] - i * BLOCK == lane, signs[...], 0.0)
    for one in early:
        one.wait()
    invert_diagonal(diag, beside, inverse, high, low)
    for c in range(CHUNKS):
        copy(c).wait()

    def block_column(k, carry):
        for c in range(SLOTS // STEP + 1):

            @pl.when(counts[k] == c)
            def _():
                m = LOADS + c * STEP
                ah, al = halves(total[k, :m])
                solved = times(nt, ah, al, high[k], low[k])
                ah, al = halves(solved)
                xh[:m], xl[:m] = ah, al
                if c:
                    product = nt(jnp.concatenate([ah, al, ah], axis=1), jnp.concatenate([ah[LOADS:], ah[LOADS:], al[LOADS:]], axis=1))
                    load[:, : c * STEP] += product[:LOADS]
                    dual[: c * STEP, : c * STEP] += product[LOADS:]

                def update(group, carry):
                    ah, al = xh[:m], xl[:m]
                    for j in range(GROUP):
                        i = BLOCKS - 1 - j - group * GROUP
                        upper = i * (2 * i + 1) + 2 * k
                        under = upper + 2 * i + 1
                        tile = jnp.concatenate(
                            [
                                jnp.concatenate([held[upper], held[upper + 1]], axis=1),
                                jnp.concatenate([held[under], held[under + 1]], axis=1),
                            ],
                            axis=0,
                        )
                        th, tl = halves(tile)
                        total[i, :m] -= times(nt, ah, al, th, tl)
                    return carry

                lax.fori_loop(0, (BLOCKS - 1 - k + GROUP - 1) // GROUP, update, 0)

        return carry

    lax.fori_loop(0, BLOCKS, block_column, 0)


def pack_gram(gram, extra):
    lane = lax.broadcasted_iota(jnp.int32, extra.shape, 1)
    gram = coarse_lanes(gram)
    columns = [pltpu.roll(gram, 24, 1)[:24], pltpu.roll(gram[16:24], 8, 1)]
    columns = jnp.concatenate(columns + [pltpu.roll(gram, 16, 1)[:24]], axis=0)
    return jnp.where(lane >= COARSE_AT + COARSE, columns, coarse_lanes(extra))


def unpack_gram(sums):
    row = lax.broadcasted_iota(jnp.int32, (LOADS, LANES), 0)
    lane = lax.broadcasted_iota(jnp.int32, (LOADS, LANES), 1)
    none = jnp.zeros((8, LANES), F32)
    known = jnp.concatenate([pltpu.roll(sums[LOADS:], 16, 1), none], axis=0)
    known = jnp.where(lane < 8, pltpu.roll(sums[:LOADS], 8, 1), known)
    last = jnp.concatenate([none, none, pltpu.roll(sums[24:LOADS], 24, 1), none], axis=0)
    known = jnp.where(lane < 16, known, jnp.where(row >= 16, last, 0.0))
    known = jnp.where((lane < 24) & (row < 24), known, 0.0)
    turned = nt(jnp.where(row == lane, 1.0, 0.0), known, HIGH)
    turned = jnp.concatenate([turned, jnp.zeros((LOADS, LANES - LOADS), F32)], axis=1)
    return jnp.where((row < 16) & (lane >= 16), turned, known)


def gram_inverse(filled):
    row = lax.broadcasted_iota(jnp.int32, (LOADS, LANES), 0)
    lane = lax.broadcasted_iota(jnp.int32, (LOADS, LANES), 1)
    filled = jnp.where((row >= CLUSTERS * MODES) & (row == lane), 1.0, filled)
    filled = jnp.where(lane == row + LOADS, 1.0, filled)
    for k in range(CLUSTERS * MODES):
        pivot = filled[k : k + 1, :] / filled[k : k + 1, k : k + 1]
        factor = jnp.where(row[:, :1] > k, filled[:, k : k + 1], 0.0)
        filled = filled - factor * pivot
    scale = jnp.sum(jnp.where(row == lane, filled, 0.0), axis=1, keepdims=True)
    lower = jnp.where((lane >= LOADS) & (lane < 2 * LOADS) & (row < CLUSTERS * MODES), filled, 0.0)
    lower = lower * lax.rsqrt(scale)
    lower = pltpu.roll(lower, COARSE_AT - LOADS, 1)
    return lax.dot_general(
        lower, lower, (((0,), (0,)), ((), ())), precision=HIGH, preferred_element_type=F32
    )


def coarse_lanes(values):
    lane = lax.broadcasted_iota(jnp.int32, values.shape, 1)
    return jnp.where((lane >= COARSE_AT) & (lane < COARSE_AT + CLUSTERS * MODES), values, 0.0)


def with_scalars(values, *scalars):
    lane = lax.broadcasted_iota(jnp.int32, values.shape, 1)
    values = coarse_lanes(values)
    for place, scalar in enumerate(scalars):
        values = jnp.where(lane == COARSE_AT + CLUSTERS * MODES + place, scalar, values)
    return values


def scalar(values, place):
    at = COARSE_AT + CLUSTERS * MODES + place
    return values[:, at : at + 1]


def rows_sum(a, b):
    return jnp.sum(a * b, axis=1, keepdims=True)


def start_kernel(
    where, table, half, sub, lower, upper, dual, load,
    modes, values, to_sub, to_lower, to_upper, picks,
):
    select_slots(table, picks)
    me, cluster = where[0], where[1]
    none = jnp.zeros((8, LANES), F32)
    within = [sub[peer_of(me, offset)[1]] for offset in FACES]
    within += [none, none] + edge_blocks(me, sub, 8)
    below = [none] * LOWER + [lower[...]] + [none] * (PLACES - LOWER - 1)
    above = [none] * UPPER + [upper[...]] + [none] * (PLACES - UPPER - 1)
    came = [jnp.concatenate(pieces, axis=1) for pieces in (within, below, above)]
    came = fold(nt(thirds(jnp.concatenate(came, axis=0)), picks[...]), 24)
    total = by_cluster(cluster, [(0, half[...] + came[:8]), (-1, came[8:16]), (1, came[16:])])
    modes[...] = jnp.concatenate([jnp.zeros((COARSE_AT, SLOTS), F32), total], axis=0)
    values[:LOADS] = load[...]
    values[LOADS:] = nn(total, dual[...], HIGH)[:COARSE]
    extra = nt(values[...], modes[...], HIGH)
    extra = pack_gram(0.5 * nt(total, modes[...], HIGH), extra)
    send_values(values[...], extra, me, picks, to_sub, to_lower, to_upper)


def pair_kernel(where, table, values, sub, lower, upper, paired, picks):
    select_slots(table, picks)
    paired[...] = values[...] + received_sum(where[0], picks, sub, lower, upper)


def first_kernel(
    where, table, s0, s1, s2, s3, coarse_load, modes, dual, paired,
    inverse, multipliers, projected, values, to_sub, to_lower, to_upper, picks,
):
    select_slots(table, picks)
    sums = (s0[...] + s1[...]) + (s2[...] + s3[...])
    inverse[...] = gram_inverse(unpack_gram(sums))
    begin = nn(coarse_load[...], inverse[...], HIGH)
    multipliers[...] = nn(begin, modes[...], HIGH)
    images = jnp.concatenate(
        [jnp.zeros((COARSE_AT, SLOTS), F32), paired[LOADS:], jnp.zeros((8, SLOTS), F32)], axis=0
    )
    residual = paired[:LOADS] - nn(begin, images, HIGH)
    sums = coarse_lanes(sums)
    curved = jnp.concatenate(
        [jnp.zeros((COARSE_AT, LANES), F32), sums[LOADS:], jnp.zeros((8, LANES), F32)], axis=0
    )
    weights = nn(sums[:LOADS] - nn(begin, curved, HIGH), inverse[...], HIGH)
    projected[...] = residual - nn(weights, modes[...], HIGH)
    values[...] = nn(projected[...], dual[...], HIGH)
    extra = with_scalars(
        nt(values[...], modes[...], HIGH),
        0.5 * rows_sum(projected[...], projected[...]),
        rows_sum(projected[...], values[...]),
    )
    send_values(values[...], extra, where[0], picks, to_sub, to_lower, to_upper)


def second_kernel(
    where, table, s0, s1, s2, s3, inverse, modes, dual, image, multipliers, projected,
    sums, moved, newer, values, to_sub, to_lower, to_upper, picks,
):
    select_slots(table, picks)
    sums[...] = (s0[...] + s1[...]) + (s2[...] + s3[...])
    alpha = scalar(sums, 0) / scalar(sums, 1)
    weights = nn(coarse_lanes(sums[...]), inverse[...], HIGH)
    moved[...] = multipliers[...] + alpha * projected[...]
    newer[...] = projected[...] - alpha * (image[...] - nn(weights, modes[...], HIGH))
    values[...] = nn(newer[...], dual[...], HIGH)
    extra = with_scalars(
        nt(values[...], modes[...], HIGH),
        0.5 * rows_sum(newer[...], newer[...]),
        rows_sum(newer[...], values[...]),
        0.5 * rows_sum(newer[...], image[...]),
    )
    send_values(values[...], extra, where[0], picks, to_sub, to_lower, to_upper)


def last_kernel(
    s0, s1, s2, s3, before, inverse, modes, paired, image, moved, projected, newer, ranks,
    multipliers_out, projected_out,
):
    sums = (s0[...] + s1[...]) + (s2[...] + s3[...])
    following = scalar(sums, 0)
    beta = following / scalar(before, 0)
    curvature = scalar(sums, 1) + beta * (2.0 * scalar(sums, 2) + beta * scalar(before, 1))
    alpha = following / curvature
    direction = newer[...] + beta * projected[...]
    image_now = paired[...] + beta * image[...]
    coarse = coarse_lanes(sums + beta * before[...])
    weights = nn(coarse, inverse[...], HIGH)
    both = jnp.concatenate(
        [
            moved[...] + alpha * direction,
            newer[...] - alpha * (image_now - nn(weights, modes[...], HIGH)),
        ],
        axis=0,
    )
    back = lax.broadcasted_iota(jnp.int32, (SLOTS, SLOTS), 0) == ranks[...]
    both = fold(nn(thirds(both), jnp.where(back, 1.0, 0.0).astype(BF16)), 2 * LOADS)
    multipliers_out[...] = both[:LOADS]
    projected_out[...] = both[LOADS:]


def shape(*dims, dtype=F32):
    return jax.ShapeDtypeStruct(dims, dtype)


def sent_shapes(rows):
    return (shape(SUBS, rows, LANES), shape(rows, LANES), shape(rows, LANES))


SENT = sent_shapes(LOADS)
VECTOR = shape(LOADS, SLOTS)
PICKS = pltpu.VMEM((SLOTS, PLACES * LANES), BF16)


def call(
    kernel, out_shape, in_specs, scratch, flops, moved, name, limit=24, out_specs=None
):
    return pl.pallas_call(
        kernel,
        out_shape=out_shape,
        in_specs=in_specs,
        out_specs=out_specs or jax.tree.map(lambda _: VMEM, out_shape),
        scratch_shapes=scratch,
        cost_estimate=pl.CostEstimate(flops=flops, bytes_accessed=moved, transcendentals=0),
        compiler_params=pltpu.CompilerParams(vmem_limit_bytes=limit << 20),
        name=name,
    )


def run_solve(counts, tiles, unknown, signs, loads):
    return call(
        solve_kernel,
        (shape(SLOTS, SLOTS), VECTOR),
        [SMEM, ANY] + [VMEM] * 3,
        [
            pltpu.VMEM(tiles.shape, F32),
            pltpu.VMEM((RHS, BLOCK), BF16),
            pltpu.VMEM((RHS, BLOCK), BF16),
            pltpu.VMEM((BLOCKS, RHS, BLOCK), F32),
            pltpu.VMEM((TILE_ROWS, TILE, TILE), F32),
            pltpu.VMEM((BLOCKS, TILE, TILE), F32),
            pltpu.VMEM((TILE_ROWS, TILE, TILE), F32),
            pltpu.VMEM((BLOCKS, BLOCK, BLOCK), BF16),
            pltpu.VMEM((BLOCKS, BLOCK, BLOCK), BF16),
            pltpu.SemaphoreType.DMA((CHUNKS,)),
            pltpu.SemaphoreType.DMA((TILE_ROWS + BLOCKS,)),
        ],
        30 << 30, 5 * SMALL, "solve", 50,
    )(counts, tiles, unknown, signs, loads)


def exchange(sent):
    to_sub, to_lower, to_upper = sent
    up = [(c, c + 1) for c in range(CLUSTERS - 1)]
    down = [(c + 1, c) for c in range(CLUSTERS - 1)]
    from_lower = lax.ppermute(to_upper, "cluster", up)
    from_upper = lax.ppermute(to_lower, "cluster", down)
    received = lax.all_to_all(to_sub, "sub", split_axis=0, concat_axis=0, tiled=True)
    return received, from_lower, from_upper


def cluster_sums(received):
    own = jnp.sum(received, axis=0)
    others = [
        lax.ppermute(own, "cluster", [(c, (c + by) % CLUSTERS) for c in range(CLUSTERS)])
        for by in (1, 2, 3)
    ]
    return (own, *others)


def local(factor_tiles, rigid_modes, load_cases, coarse_load, peer_slots, slot_unknown):
    cluster = lax.axis_index("cluster")
    me = lax.axis_index("sub")
    where = jnp.stack([me, cluster]).astype(jnp.int32)

    table, unknown, signs, ranks, counts, half, *sent = call(
        prepare_kernel,
        (
            shape(8, PLACES * LANES, dtype=jnp.int32),
            shape(SLOTS, 1, dtype=jnp.int32),
            shape(SLOTS, 1),
            shape(1, SLOTS, dtype=jnp.int32),
            shape(16, dtype=jnp.int32),
            shape(8, SLOTS),
            *sent_shapes(8),
        ),
        [SMEM, VMEM, VMEM, VMEM],
        [pltpu.VMEM((CLUSTERS * SUBS, LANES), jnp.int32), PICKS],
        1 << 30, SMALL, "prepare",
        out_specs=(VMEM, VMEM, VMEM, VMEM, SMEM, VMEM, VMEM, VMEM, VMEM),
    )(where, peer_slots[0].T, slot_unknown, jnp.swapaxes(rigid_modes, 0, 1))
    received = exchange(sent)
    dual, load = run_solve(counts, factor_tiles[0], unknown, signs, load_cases[0])

    modes, values, *sent = call(
        start_kernel,
        (shape(LANES, SLOTS), shape(ROWS, SLOTS), *sent_shapes(ROWS)),
        [SMEM] + [VMEM] * 7,
        [PICKS], 1 << 30, SMALL, "start",
    )(where, table, half, *received, dual, load)

    def meet(values, sent):
        received = exchange(sent)
        sums = cluster_sums(received[0])
        paired = call(
            pair_kernel,
            shape(*values.shape),
            [SMEM] + [VMEM] * 5,
            [PICKS], 1 << 30, SMALL, "pair",
        )(where, table, values, *received)
        return sums, paired

    sums, paired = meet(values, sent)
    spread_load = jnp.pad(
        coarse_load.T, ((0, 0), (COARSE_AT, LANES - COARSE_AT - CLUSTERS * MODES))
    )
    inverse, multipliers, projected, values, *sent = call(
        first_kernel,
        (shape(LANES, LANES), VECTOR, VECTOR, VECTOR, *SENT),
        [SMEM] + [VMEM] * 9,
        [PICKS], 1 << 30, SMALL, "first",
    )(where, table, *sums, spread_load, modes, dual, paired)
    sums, image = meet(values, sent)
    before, moved, newer, values, *sent = call(
        second_kernel,
        (shape(LOADS, LANES), VECTOR, VECTOR, VECTOR, *SENT),
        [SMEM] + [VMEM] * 11,
        [PICKS], 1 << 30, SMALL, "second",
    )(where, table, *sums, inverse, modes, dual, image, multipliers, projected)
    sums, paired = meet(values, sent)
    multipliers, projected = call(
        last_kernel,
        (VECTOR, VECTOR),
        [VMEM] * 13,
        [], 1 << 30, SMALL, "last",
    )(*sums, before, inverse, modes, paired, image, moved, projected, newer, ranks)
    return (multipliers.T[None], projected.T[None])


def solution(mesh):
    return jax.shard_map(
        local,
        mesh=mesh,
        in_specs=(
            P(("cluster", "sub"), None, None, None),
            P(("cluster", "sub"), None, None),
            P(("cluster", "sub"), None, None),
            P(),
            P(("cluster", "sub"), None, None),
            P(("cluster", "sub"), None),
        ),
        out_specs=(P(("cluster", "sub"), None, None), P(("cluster", "sub"), None, None)),
        check_vma=False,
    )
```

```python
import functools

import jax
import jax.numpy as jnp
from jax import lax
from jax.experimental import pallas as pl
from jax.experimental.pallas import tpu as pltpu
from jax.sharding import PartitionSpec as P

F32 = jnp.float32
BF16 = jnp.bfloat16
HIGH = lax.Precision.HIGHEST

UNKNOWNS = 3072
SLOTS = 640
LOADS = 32
RHS = SLOTS + LOADS
TILE = 128
TILE_ROWS = 24
BLOCK = 256
BLOCKS = UNKNOWNS // BLOCK
SUBS = 32
CLUSTERS = 4
MODES = 6
COARSE = CLUSTERS * MODES
ROWS = LOADS + COARSE
LANES = 128
COARSE_AT = 96
FACES = [(0, 0, 1), (0, 0, -1), (0, 1, 0), (0, -1, 0), (1, 0, 0)]
EDGES = [(0, 1, 1), (0, 1, -1), (1, 0, 1), (1, 1, 0), (1, 1, 1), (1, 1, -1)]
SLOT, EDGE_MOST = 16, 12
LOWER, UPPER, EDGE = len(FACES), len(FACES) + 1, len(FACES) + 2
PLACES = len(FACES) + 4
SMALL = 1 << 22
CHUNK = 12
CHUNKS = 25
STEP = 128
GROUP = 4
VMEM = pl.BlockSpec(memory_space=pltpu.VMEM)
SMEM = pl.BlockSpec(memory_space=pltpu.SMEM)
ANY = pl.BlockSpec(memory_space=pl.ANY)
HBM = pl.BlockSpec(memory_space=pltpu.HBM)


def nt(a, b, precision=None):
    return lax.dot_general(
        a, b, (((1,), (1,)), ((), ())), precision=precision, preferred_element_type=F32
    )


def nn(a, b, precision=None):
    return lax.dot_general(
        a, b, (((1,), (0,)), ((), ())), precision=precision, preferred_element_type=F32
    )


def halves(a):
    high = a.astype(BF16)
    return high, (a - high.astype(F32)).astype(BF16)


def thirds(a):
    high = a.astype(BF16).astype(F32)
    rest = a - high
    middle = rest.astype(BF16).astype(F32)
    return jnp.concatenate([high, middle, rest - middle], axis=0).astype(BF16)


def fold(a, rows):
    return a[:rows] + a[rows : 2 * rows] + a[2 * rows :]


def times(dot, high, low, right_high, right_low):
    m = high.shape[0]
    product = dot(jnp.concatenate([high, low], axis=0), right_high)
    return product[:m] + product[m:] + dot(high, right_low)


def mm(a, b):
    return times(nn, *halves(a), *halves(b))


def opposite(offset):
    return (offset[0], -offset[1], -offset[2])


def peer_of(me, offset):
    dz, dx, dy = offset
    z, x, y = me // 16, (me // 4) % 4 + dx, me % 4 + dy
    valid = (x >= 0) & (x < 4) & (y >= 0) & (y < 4)
    return valid, jnp.where(valid, (1 - z if dz else z) * 16 + x * 4 + y, me)


def edges():
    for side in (0, 1):
        for slot, offset in enumerate(EDGES):
            yield side, slot, opposite(offset) if side else offset


def in_slot(shape, slot):
    lane = lax.broadcasted_iota(jnp.int32, shape, 1)
    return (lane >= slot * SLOT) & (lane < slot * SLOT + EDGE_MOST)


def lanes_of(values, place):
    return values[:, place * LANES : (place + 1) * LANES]


def pick(picks, place, wanted):
    slot = lax.broadcasted_iota(jnp.int32, (SLOTS, LANES), 0)
    at = pl.ds(pl.multiple_of(place * LANES, LANES), LANES)
    picks[:, at] = jnp.where(slot == wanted, 1.0, 0.0).astype(BF16)


def select_slots(table, picks):
    def one(place, carry):
        at = pl.ds(pl.multiple_of(place * LANES, LANES), LANES)
        pick(picks, place, table[:1, at])
        return carry

    lax.fori_loop(0, PLACES, one, 0)


def send_values(values, extra, me, picks, to_sub, to_lower, to_upper):
    rows = values.shape[0]
    for peer in range(SUBS):
        to_sub[peer] = extra
    picked = fold(nn(thirds(values), picks[...]), rows)
    for place, offset in enumerate(FACES):
        valid, peer = peer_of(me, offset)

        @pl.when(valid)
        def _():
            to_sub[peer] = lanes_of(picked, place) + extra

    for side, slot, offset in edges():
        valid, peer = peer_of(me, offset)

        @pl.when(valid)
        def _():
            mine = lanes_of(picked, EDGE + side)
            to_sub[peer] = jnp.where(in_slot(mine.shape, slot), mine, extra)

    to_lower[...] = lanes_of(picked, LOWER)
    to_upper[...] = lanes_of(picked, UPPER)


def edge_blocks(me, sub, rows):
    blocks = [jnp.zeros((rows, LANES), F32)] * 2
    for side, slot, offset in edges():
        came = sub[peer_of(me, offset)[1]][:rows]
        blocks[side] = jnp.where(in_slot((rows, LANES), slot), came, blocks[side])
    return blocks


def received_sum(me, picks, sub, lower, upper):
    rows = lower.shape[0]
    pieces = [sub[peer_of(me, offset)[1]] for offset in FACES]
    pieces += [lower[...], upper[...]] + edge_blocks(me, sub, rows)
    return fold(nt(thirds(jnp.concatenate(pieces, axis=1)), picks[...]), rows)


def by_cluster(cluster, parts):
    row = lax.broadcasted_iota(jnp.int32, (LOADS, SLOTS), 0)
    placed = jnp.zeros((LOADS, SLOTS), F32)
    for step, part in parts:
        for mode in range(MODES):
            at = (cluster + step) * MODES + mode
            placed = placed + jnp.where(row == at, part[mode : mode + 1, :], 0.0)
    return placed


def prepare_kernel(
    where, peer_slots_hbm, unknown_hbm, rigid_hbm,
    table, sorted_unknown, signs, ranks, counts, half, to_sub, to_lower, to_upper,
    peer_table, picks, peer_slots, unknown_row, rigid, sems,
):
    me, cluster = where[0], where[1]
    copies = [
        pltpu.make_async_copy(peer_slots_hbm, peer_slots, sems.at[0]),
        pltpu.make_async_copy(unknown_hbm, unknown_row, sems.at[1]),
        pltpu.make_async_copy(rigid_hbm, rigid, sems.at[2]),
    ]
    for copy in copies:
        copy.start()
    for copy in copies:
        copy.wait()
    devices = peer_slots.shape[1]
    listed = jnp.concatenate(
        [
            peer_slots[...].astype(F32),
            jnp.full((LANES - peer_slots.shape[0], devices), float(SLOTS), F32),
        ],
        axis=0,
    )
    peer_table[...] = jnp.transpose(listed).astype(jnp.int32)
    base = cluster * SUBS
    own = base + me

    def wanted_of(valid, row):
        return jnp.where(valid, peer_table[pl.ds(row, 1), :], SLOTS)

    ups = []
    for place, offset in enumerate(FACES):
        valid, peer = peer_of(me, offset)
        pick(picks, place, wanted_of(valid, base + peer))
        ups.append(jnp.full((8, LANES), jnp.where(peer > me, 1.0, -1.0), F32))
    pick(picks, LOWER, wanted_of(own >= SUBS, jnp.maximum(own - SUBS, 0)))
    pick(picks, UPPER, wanted_of(own + SUBS < devices, jnp.minimum(own + SUBS, devices - 1)))
    ups += [jnp.full((8, LANES), -1.0, F32), jnp.full((8, LANES), 1.0, F32)]
    wanted = [jnp.full((1, LANES), SLOTS, jnp.int32)] * 2
    signs_of = [jnp.full((8, LANES), 1.0, F32)] * 2
    for side, slot, offset in edges():
        valid, peer = peer_of(me, offset)
        row = wanted_of(valid, base + peer)
        row = pltpu.roll(row, slot * SLOT, 1) if slot else row
        wanted[side] = jnp.where(in_slot((1, LANES), slot), row, wanted[side])
        signs_of[side] = jnp.where(
            in_slot((8, LANES), slot), jnp.where(peer > me, 1.0, -1.0), signs_of[side]
        )
    pick(picks, EDGE, wanted[0])
    pick(picks, EDGE + 1, wanted[1])
    ups = jnp.concatenate(ups + signs_of, axis=1)
    across = lax.broadcasted_iota(jnp.int32, (1, SLOTS), 1)
    key_row = unknown_row[...] * 1024 + across
    key_column = jnp.transpose(jnp.broadcast_to(key_row.astype(F32), (8, SLOTS)))[:, :1]
    key_column = key_column.astype(jnp.int32)
    rank = jnp.sum(jnp.where(key_column < key_row, 1.0, 0.0), axis=0, keepdims=True)
    rank_int = rank.astype(jnp.int32)
    ranks[...] = rank_int
    row = lax.broadcasted_iota(jnp.int32, (8, SLOTS), 0)
    coarse_rank = jnp.right_shift(rank_int, 8)
    digits = jnp.where(row == 0, coarse_rank, jnp.where(row == 1, rank_int - coarse_rank * 256, 1))
    moved = nn(digits.astype(F32).astype(BF16), picks[...])
    moved = moved[:1] * 256.0 + moved[1:2] + (1.0 - moved[2:3]) * 1024.0
    table[...] = jnp.broadcast_to(moved.astype(jnp.int32), (8, PLACES * LANES))
    sign_row = nt(ups.astype(BF16), picks[...])[:1]
    unknown_float = unknown_row[...].astype(F32)
    for start in range(0, SLOTS, LANES):
        match = lax.broadcasted_iota(jnp.int32, (LANES, SLOTS), 0) + start == rank_int
        at = slice(start, start + LANES)
        sorted_unknown[at] = jnp.sum(
            jnp.where(match, unknown_float, 0.0), axis=1, keepdims=True
        ).astype(jnp.int32)
        signs[at] = jnp.sum(jnp.where(match, sign_row, 0.0), axis=1, keepdims=True)
    for block in range(BLOCKS):
        within = jnp.where(unknown_row[...] < (block + 1) * BLOCK, 1.0, 0.0)
        counts[block] = (jnp.sum(within).astype(jnp.int32) + STEP - 1) // STEP
    select_slots(table, picks)
    own = jnp.zeros((24, SLOTS), F32)
    lane = lax.broadcasted_iota(jnp.int32, (SLOTS, BLOCK), 1)
    for block in range(BLOCKS):
        rows = [rigid[mode, :, block * BLOCK : (block + 1) * BLOCK] for mode in range(MODES)]
        rows = jnp.concatenate(rows + [jnp.zeros((8 - MODES, BLOCK), F32)], axis=0)
        glue = jnp.where(sorted_unknown[...] - block * BLOCK == lane, signs[...], 0.0).astype(BF16)
        own = own + nt(thirds(rows), glue)
    own = fold(own, 8)
    half[...] = own
    send_values(own, jnp.zeros((8, LANES), F32), me, picks, to_sub, to_lower, to_upper)


def invert_diagonal(diag, beside, inverse, high, low):
    base, group, some, many = 32, 8, 12, 24
    lane3 = lax.broadcasted_iota(jnp.int32, (some, group, TILE), 2)
    row = lax.broadcasted_iota(jnp.int32, (some, group, TILE), 1)
    flat_lane = lax.broadcasted_iota(jnp.int32, (some * group, TILE), 1)

    def substitute(step, carry):
        tiles = pl.ds(step * some, some)
        given, solved = [], []
        for g in range(base // group):
            block = jnp.zeros((some, group, TILE), F32)
            for b in range(TILE // base):
                at = b * base + g * group
                block = jnp.where(lane3 // base == b, diag[tiles, at : at + group, :], block)
            given.append(block.reshape(some * group, TILE))
            solved.append(jnp.where(row + g * group == lane3 % base, 1.0, 0.0))
        for k in range(base):
            now, at = k // group, k % group
            column = [None] * (base // group)
            for g in range(now, base // group):
                column[g] = jnp.take_along_axis(
                    given[g], flat_lane // base * base + k, axis=1, mode="promise_in_bounds"
                ).reshape(some, group, TILE)
            pivot = solved[now][:, at : at + 1, :] / column[now][:, at : at + 1, :]
            solved[now] = jnp.where(
                row == at,
                pivot,
                jnp.where(row > at, solved[now] - column[now] * pivot, solved[now]),
            )
            for g in range(now + 1, base // group):
                solved[g] = solved[g] - column[g] * pivot
        for g in range(base // group):
            for b in range(TILE // base):
                at = b * base + g * group
                inverse[tiles, at : at + group, :] = jnp.where(lane3 // base == b, solved[g], 0.0)
        return carry

    lax.fori_loop(0, TILE_ROWS // some, substitute, 0)
    half, quarter = TILE // 2, TILE // 4
    odd = [slice(quarter, half), slice(half + quarter, TILE)]
    lane = lax.broadcasted_iota(jnp.int32, (quarter, TILE), 1)
    none = jnp.zeros((quarter, TILE), F32)

    def merge_quarters(step, carry):
        for n in range(many):
            t = step * many + n
            below = [
                jnp.where(lane < quarter, diag[t, odd[0], :], 0.0),
                jnp.where((lane >= half) & (lane < half + quarter), diag[t, odd[1], :], 0.0),
            ]
            partial = mm(jnp.concatenate(below, axis=0), inverse[t])
            partial = jnp.concatenate([none, partial[:quarter], none, partial[quarter:]], axis=0)
            rows = jnp.concatenate([inverse[t, odd[0], :], inverse[t, odd[1], :]], axis=0)
            rows = rows - mm(rows, partial)
            inverse[t, odd[0], :] = rows[:quarter]
            inverse[t, odd[1], :] = rows[quarter:]
        return carry

    lax.fori_loop(0, TILE_ROWS // many, merge_quarters, 0)

    def merge_halves(step, carry):
        for n in range(many):
            t = step * many + n
            partial = mm(diag[t, half:, :half], inverse[t, :half, :half])
            inverse[t, half:, :half] = -mm(inverse[t, half:, half:], partial)
        return carry

    lax.fori_loop(0, TILE_ROWS // many, merge_halves, 0)

    def merge_tiles(step, carry):
        for n in range(many // 2):
            j = step * (many // 2) + n
            first, second = inverse[2 * j], inverse[2 * j + 1]
            off = -mm(second, mm(beside[j], first))
            whole = jnp.concatenate(
                [
                    jnp.concatenate([first, jnp.zeros((TILE, TILE), F32)], axis=1),
                    jnp.concatenate([off, second], axis=1),
                ],
                axis=0,
            )
            high[j], low[j] = halves(whole)
        return carry

    lax.fori_loop(0, 2 * BLOCKS // many, merge_tiles, 0)


def solve_kernel(
    counts, tiles, unknown, signs, loads_hbm, dual, load,
    loads, held, xh, xl, total, diag, beside, inverse, high, low, sems, early_sems, load_sem,
):
    def copy(c):
        at = pl.ds(c * CHUNK, CHUNK)
        return pltpu.make_async_copy(tiles.at[at], held.at[at], sems.at[c])

    early = [pltpu.make_async_copy(loads_hbm, loads, load_sem.at[0])]
    for t in range(TILE_ROWS):
        at = t * (t + 1) // 2 + t
        early.append(pltpu.make_async_copy(tiles.at[at], diag.at[t], early_sems.at[t]))
        if t % 2:
            early.append(
                pltpu.make_async_copy(
                    tiles.at[at - 1], beside.at[t // 2], early_sems.at[TILE_ROWS + t // 2]
                )
            )
    for one in early:
        one.start()
    for c in range(CHUNKS):
        copy(c).start()
    dual[...] = jnp.zeros_like(dual)
    load[...] = jnp.zeros_like(load)
    for one in early:
        one.wait()
    lane = lax.broadcasted_iota(jnp.int32, (SLOTS, BLOCK), 1)
    for i in range(BLOCKS):
        total[i, :LOADS] = loads[:, i * BLOCK : (i + 1) * BLOCK]
        total[i, LOADS:] = jnp.where(unknown[...] - i * BLOCK == lane, signs[...], 0.0)
    invert_diagonal(diag, beside, inverse, high, low)
    for c in range(CHUNKS):
        copy(c).wait()

    def block_column(k, carry):
        for c in range(SLOTS // STEP + 1):

            @pl.when(counts[k] == c)
            def _():
                m = LOADS + c * STEP
                ah, al = halves(total[k, :m])
                solved = times(nt, ah, al, high[k], low[k])
                ah, al = halves(solved)
                xh[:m], xl[:m] = ah, al
                if c:
                    product = nt(jnp.concatenate([ah, al, ah], axis=1), jnp.concatenate([ah[LOADS:], ah[LOADS:], al[LOADS:]], axis=1))
                    load[:, : c * STEP] += product[:LOADS]
                    dual[: c * STEP, : c * STEP] += product[LOADS:]

                def update(group, carry):
                    ah, al = xh[:m], xl[:m]
                    for j in range(GROUP):
                        i = BLOCKS - 1 - j - group * GROUP
                        upper = i * (2 * i + 1) + 2 * k
                        under = upper + 2 * i + 1
                        tile = jnp.concatenate(
                            [
                                jnp.concatenate([held[upper], held[upper + 1]], axis=1),
                                jnp.concatenate([held[under], held[under + 1]], axis=1),
                            ],
                            axis=0,
                        )
                        th, tl = halves(tile)
                        total[i, :m] -= times(nt, ah, al, th, tl)
                    return carry

                lax.fori_loop(0, (BLOCKS - 1 - k + GROUP - 1) // GROUP, update, 0)

        return carry

    lax.fori_loop(0, BLOCKS, block_column, 0)


def pack_gram(gram, extra):
    lane = lax.broadcasted_iota(jnp.int32, extra.shape, 1)
    gram = coarse_lanes(gram)
    columns = [pltpu.roll(gram, 24, 1)[:24], pltpu.roll(gram[16:24], 8, 1)]
    columns = jnp.concatenate(columns + [pltpu.roll(gram, 16, 1)[:24]], axis=0)
    return jnp.where(lane >= COARSE_AT + COARSE, columns, coarse_lanes(extra))


def unpack_gram(sums):
    row = lax.broadcasted_iota(jnp.int32, (LOADS, LANES), 0)
    lane = lax.broadcasted_iota(jnp.int32, (LOADS, LANES), 1)
    none = jnp.zeros((8, LANES), F32)
    known = jnp.concatenate([pltpu.roll(sums[LOADS:], 16, 1), none], axis=0)
    known = jnp.where(lane < 8, pltpu.roll(sums[:LOADS], 8, 1), known)
    last = jnp.concatenate([none, none, pltpu.roll(sums[24:LOADS], 24, 1), none], axis=0)
    known = jnp.where(lane < 16, known, jnp.where(row >= 16, last, 0.0))
    known = jnp.where((lane < 24) & (row < 24), known, 0.0)
    turned = nt(jnp.where(row == lane, 1.0, 0.0), known, HIGH)
    turned = jnp.concatenate([turned, jnp.zeros((LOADS, LANES - LOADS), F32)], axis=1)
    return jnp.where((row < 16) & (lane >= 16), turned, known)


def gram_inverse(filled):
    row = lax.broadcasted_iota(jnp.int32, (LOADS, LANES), 0)
    lane = lax.broadcasted_iota(jnp.int32, (LOADS, LANES), 1)
    filled = jnp.where((row >= CLUSTERS * MODES) & (row == lane), 1.0, filled)
    filled = jnp.where(lane == row + LOADS, 1.0, filled)
    for k in range(CLUSTERS * MODES):
        pivot = filled[k : k + 1, :] / filled[k : k + 1, k : k + 1]
        factor = jnp.where(row[:, :1] > k, filled[:, k : k + 1], 0.0)
        filled = filled - factor * pivot
    scale = jnp.sum(jnp.where(row == lane, filled, 0.0), axis=1, keepdims=True)
    lower = jnp.where((lane >= LOADS) & (lane < 2 * LOADS) & (row < CLUSTERS * MODES), filled, 0.0)
    lower = lower * lax.rsqrt(scale)
    lower = pltpu.roll(lower, COARSE_AT - LOADS, 1)
    return lax.dot_general(
        lower, lower, (((0,), (0,)), ((), ())), precision=HIGH, preferred_element_type=F32
    )


def coarse_lanes(values):
    lane = lax.broadcasted_iota(jnp.int32, values.shape, 1)
    return jnp.where((lane >= COARSE_AT) & (lane < COARSE_AT + CLUSTERS * MODES), values, 0.0)


def with_scalars(values, *scalars):
    lane = lax.broadcasted_iota(jnp.int32, values.shape, 1)
    values = coarse_lanes(values)
    for place, scalar in enumerate(scalars):
        values = jnp.where(lane == COARSE_AT + CLUSTERS * MODES + place, scalar, values)
    return values


def scalar(values, place):
    at = COARSE_AT + CLUSTERS * MODES + place
    return values[:, at : at + 1]


def rows_sum(a, b):
    return jnp.sum(a * b, axis=1, keepdims=True)


def start_kernel(
    where, table, half, sub, lower, upper, dual, load,
    modes, values, to_sub, to_lower, to_upper, picks,
):
    select_slots(table, picks)
    me, cluster = where[0], where[1]
    none = jnp.zeros((8, LANES), F32)
    within = [sub[peer_of(me, offset)[1]] for offset in FACES]
    within += [none, none] + edge_blocks(me, sub, 8)
    below = [none] * LOWER + [lower[...]] + [none] * (PLACES - LOWER - 1)
    above = [none] * UPPER + [upper[...]] + [none] * (PLACES - UPPER - 1)
    came = [jnp.concatenate(pieces, axis=1) for pieces in (within, below, above)]
    came = fold(nt(thirds(jnp.concatenate(came, axis=0)), picks[...]), 24)
    total = by_cluster(cluster, [(0, half[...] + came[:8]), (-1, came[8:16]), (1, came[16:])])
    modes[...] = jnp.concatenate([jnp.zeros((COARSE_AT, SLOTS), F32), total], axis=0)
    values[:LOADS] = load[...]
    values[LOADS:] = nn(total, dual[...], HIGH)[:COARSE]
    extra = nt(values[...], modes[...], HIGH)
    extra = pack_gram(0.5 * nt(total, modes[...], HIGH), extra)
    send_values(values[...], extra, me, picks, to_sub, to_lower, to_upper)


def pair_kernel(where, table, values, sub, lower, upper, paired, picks):
    select_slots(table, picks)
    paired[...] = values[...] + received_sum(where[0], picks, sub, lower, upper)


def first_kernel(
    where, table, s0, s1, s2, s3, coarse_load, modes, dual, paired,
    inverse, multipliers, projected, values, to_sub, to_lower, to_upper, picks,
):
    select_slots(table, picks)
    sums = (s0[...] + s1[...]) + (s2[...] + s3[...])
    inverse[...] = gram_inverse(unpack_gram(sums))
    begin = nn(coarse_load[...], inverse[...], HIGH)
    multipliers[...] = nn(begin, modes[...], HIGH)
    images = jnp.concatenate(
        [jnp.zeros((COARSE_AT, SLOTS), F32), paired[LOADS:], jnp.zeros((8, SLOTS), F32)], axis=0
    )
    residual = paired[:LOADS] - nn(begin, images, HIGH)
    sums = coarse_lanes(sums)
    curved = jnp.concatenate(
        [jnp.zeros((COARSE_AT, LANES), F32), sums[LOADS:], jnp.zeros((8, LANES), F32)], axis=0
    )
    weights = nn(sums[:LOADS] - nn(begin, curved, HIGH), inverse[...], HIGH)
    projected[...] = residual - nn(weights, modes[...], HIGH)
    values[...] = nn(projected[...], dual[...], HIGH)
    extra = with_scalars(
        nt(values[...], modes[...], HIGH),
        0.5 * rows_sum(projected[...], projected[...]),
        rows_sum(projected[...], values[...]),
    )
    send_values(values[...], extra, where[0], picks, to_sub, to_lower, to_upper)


def second_kernel(
    where, table, s0, s1, s2, s3, inverse, modes, dual, image, multipliers, projected,
    sums, moved, newer, values, to_sub, to_lower, to_upper, picks,
):
    select_slots(table, picks)
    sums[...] = (s0[...] + s1[...]) + (s2[...] + s3[...])
    alpha = scalar(sums, 0) / scalar(sums, 1)
    weights = nn(coarse_lanes(sums[...]), inverse[...], HIGH)
    moved[...] = multipliers[...] + alpha * projected[...]
    newer[...] = projected[...] - alpha * (image[...] - nn(weights, modes[...], HIGH))
    values[...] = nn(newer[...], dual[...], HIGH)
    extra = with_scalars(
        nt(values[...], modes[...], HIGH),
        0.5 * rows_sum(newer[...], newer[...]),
        rows_sum(newer[...], values[...]),
        0.5 * rows_sum(newer[...], image[...]),
    )
    send_values(values[...], extra, where[0], picks, to_sub, to_lower, to_upper)


def last_kernel(
    s0, s1, s2, s3, before, inverse, modes, paired, image, moved, projected, newer, ranks,
    multipliers_out, projected_out,
):
    sums = (s0[...] + s1[...]) + (s2[...] + s3[...])
    following = scalar(sums, 0)
    beta = following / scalar(before, 0)
    curvature = scalar(sums, 1) + beta * (2.0 * scalar(sums, 2) + beta * scalar(before, 1))
    alpha = following / curvature
    direction = newer[...] + beta * projected[...]
    image_now = paired[...] + beta * image[...]
    coarse = coarse_lanes(sums + beta * before[...])
    weights = nn(coarse, inverse[...], HIGH)
    both = jnp.concatenate(
        [
            moved[...] + alpha * direction,
            newer[...] - alpha * (image_now - nn(weights, modes[...], HIGH)),
        ],
        axis=0,
    )
    back = lax.broadcasted_iota(jnp.int32, (SLOTS, SLOTS), 0) == ranks[...]
    both = fold(nn(thirds(both), jnp.where(back, 1.0, 0.0).astype(BF16)), 2 * LOADS)
    multipliers_out[...] = both[:LOADS]
    projected_out[...] = both[LOADS:]


def shape(*dims, dtype=F32):
    return jax.ShapeDtypeStruct(dims, dtype)


def sent_shapes(rows):
    return (shape(SUBS, rows, LANES), shape(rows, LANES), shape(rows, LANES))


SENT = sent_shapes(LOADS)
VECTOR = shape(LOADS, SLOTS)
PICKS = pltpu.VMEM((SLOTS, PLACES * LANES), BF16)


def call(
    kernel, out_shape, in_specs, scratch, flops, moved, name, limit=24, out_specs=None
):
    return pl.pallas_call(
        kernel,
        out_shape=out_shape,
        in_specs=in_specs,
        out_specs=out_specs or jax.tree.map(lambda _: VMEM, out_shape),
        scratch_shapes=scratch,
        cost_estimate=pl.CostEstimate(flops=flops, bytes_accessed=moved, transcendentals=0),
        compiler_params=pltpu.CompilerParams(vmem_limit_bytes=limit << 20),
        name=name,
    )


def run_solve(counts, tiles, unknown, signs, loads):
    return call(
        solve_kernel,
        (shape(SLOTS, SLOTS), VECTOR),
        [SMEM, ANY, VMEM, VMEM, HBM],
        [
            pltpu.VMEM((LOADS, UNKNOWNS), F32),
            pltpu.VMEM(tiles.shape, F32),
            pltpu.VMEM((RHS, BLOCK), BF16),
            pltpu.VMEM((RHS, BLOCK), BF16),
            pltpu.VMEM((BLOCKS, RHS, BLOCK), F32),
            pltpu.VMEM((TILE_ROWS, TILE, TILE), F32),
            pltpu.VMEM((BLOCKS, TILE, TILE), F32),
            pltpu.VMEM((TILE_ROWS, TILE, TILE), F32),
            pltpu.VMEM((BLOCKS, BLOCK, BLOCK), BF16),
            pltpu.VMEM((BLOCKS, BLOCK, BLOCK), BF16),
            pltpu.SemaphoreType.DMA((CHUNKS,)),
            pltpu.SemaphoreType.DMA((TILE_ROWS + BLOCKS,)),
            pltpu.SemaphoreType.DMA((1,)),
        ],
        30 << 30, 5 * SMALL, "solve", 50,
    )(counts, tiles, unknown, signs, loads)


def exchange(sent):
    to_sub, to_lower, to_upper = sent
    up = [(c, c + 1) for c in range(CLUSTERS - 1)]
    down = [(c + 1, c) for c in range(CLUSTERS - 1)]
    from_lower = lax.ppermute(to_upper, "cluster", up)
    from_upper = lax.ppermute(to_lower, "cluster", down)
    received = lax.all_to_all(to_sub, "sub", split_axis=0, concat_axis=0, tiled=True)
    return received, from_lower, from_upper


def cluster_sums(received):
    own = jnp.sum(received, axis=0)
    others = [
        lax.ppermute(own, "cluster", [(c, (c + by) % CLUSTERS) for c in range(CLUSTERS)])
        for by in (1, 2, 3)
    ]
    return (own, *others)


def local(factor_tiles, rigid_modes, load_cases, coarse_load, peer_slots, slot_unknown):
    cluster = lax.axis_index("cluster")
    me = lax.axis_index("sub")
    where = jnp.stack([me, cluster]).astype(jnp.int32)

    table, unknown, signs, ranks, counts, half, *sent = call(
        prepare_kernel,
        (
            shape(8, PLACES * LANES, dtype=jnp.int32),
            shape(SLOTS, 1, dtype=jnp.int32),
            shape(SLOTS, 1),
            shape(1, SLOTS, dtype=jnp.int32),
            shape(16, dtype=jnp.int32),
            shape(8, SLOTS),
            *sent_shapes(8),
        ),
        [SMEM, HBM, HBM, HBM],
        [
            pltpu.VMEM((CLUSTERS * SUBS, LANES), jnp.int32),
            PICKS,
            pltpu.VMEM(peer_slots.shape[:0:-1], jnp.int32),
            pltpu.VMEM(slot_unknown.shape, jnp.int32),
            pltpu.VMEM((MODES, 1, UNKNOWNS), F32),
            pltpu.SemaphoreType.DMA((3,)),
        ],
        1 << 30, SMALL, "prepare", 60,
        out_specs=(VMEM, VMEM, VMEM, VMEM, SMEM, VMEM, VMEM, VMEM, VMEM),
    )(where, peer_slots[0].T, slot_unknown, jnp.swapaxes(rigid_modes, 0, 1))
    received = exchange(sent)
    dual, load = run_solve(counts, factor_tiles[0], unknown, signs, load_cases[0])

    modes, values, *sent = call(
        start_kernel,
        (shape(LANES, SLOTS), shape(ROWS, SLOTS), *sent_shapes(ROWS)),
        [SMEM] + [VMEM] * 7,
        [PICKS], 1 << 30, SMALL, "start",
    )(where, table, half, *received, dual, load)

    def meet(values, sent):
        received = exchange(sent)
        sums = cluster_sums(received[0])
        paired = call(
            pair_kernel,
            shape(*values.shape),
            [SMEM] + [VMEM] * 5,
            [PICKS], 1 << 30, SMALL, "pair",
        )(where, table, values, *received)
        return sums, paired

    sums, paired = meet(values, sent)
    spread_load = jnp.pad(
        coarse_load.T, ((0, 0), (COARSE_AT, LANES - COARSE_AT - CLUSTERS * MODES))
    )
    inverse, multipliers, projected, values, *sent = call(
        first_kernel,
        (shape(LANES, LANES), VECTOR, VECTOR, VECTOR, *SENT),
        [SMEM] + [VMEM] * 9,
        [PICKS], 1 << 30, SMALL, "first",
    )(where, table, *sums, spread_load, modes, dual, paired)
    sums, image = meet(values, sent)
    before, moved, newer, values, *sent = call(
        second_kernel,
        (shape(LOADS, LANES), VECTOR, VECTOR, VECTOR, *SENT),
        [SMEM] + [VMEM] * 11,
        [PICKS], 1 << 30, SMALL, "second",
    )(where, table, *sums, inverse, modes, dual, image, multipliers, projected)
    sums, paired = meet(values, sent)
    multipliers, projected = call(
        last_kernel,
        (VECTOR, VECTOR),
        [VMEM] * 13,
        [], 1 << 30, SMALL, "last",
    )(*sums, before, inverse, modes, paired, image, moved, projected, newer, ranks)
    return (multipliers.T[None], projected.T[None])


def solution(mesh):
    return jax.shard_map(
        local,
        mesh=mesh,
        in_specs=(
            P(("cluster", "sub"), None, None, None),
            P(("cluster", "sub"), None, None),
            P(("cluster", "sub"), None, None),
            P(),
            P(("cluster", "sub"), None, None),
            P(("cluster", "sub"), None),
        ),
        out_specs=(P(("cluster", "sub"), None, None), P(("cluster", "sub"), None, None)),
        check_vma=False,
    )
```
